32 devices in a mesh: groups: 2 (over x), elec: 8 (over z, y), walk: 2 (over core).
Axes of the slice: x: 2, y: 2, z: 4, core: 2. Of those that a mesh axis runs over, the one named last changes fastest.
Arguments:
- hidden: bfloat16 [16, 128, 256], P(('groups', 'walk'), 'elec'), parts along dimension 0, may hold values from -6 to 6
- cotangent: bfloat16 [16, 128, 256], P(('groups', 'walk'), 'elec'), parts along dimension 0, may hold values from -6 to 6
- positions: float32 [16, 3, 128], P(('groups', 'walk'), None, 'elec'), parts along dimension 0, may hold values from 0 to 1
- spins: int32 [256], P(('groups', 'elec')), parts along dimension 0, may hold values from 0 to 1
- w_in: bfloat16 [256, 32], replicated, may hold values from -0.375 to 0.375
- w_pair: float32 [32, 32], replicated, may hold values from -1 to 1
- spin_bias: float32 [2, 32], replicated, may hold values from -3 to 3
- rates: float32 [32], replicated, may hold values from 1 to 100
- w_out: bfloat16 [32, 256], replicated, may hold values from -1 to 1
Outputs:
- hidden_grad: bfloat16 [16, 128, 256], P(('groups', 'walk'), 'elec'), parts along dimension 0
- w_in_grad: float32 [512, 32], P('groups'), parts along dimension 0
- w_pair_grad: float32 [64, 32], P('groups'), parts along dimension 0
- spin_bias_grad: float32 [4, 32], P('groups'), parts along dimension 0
- w_out_grad: float32 [64, 256], P('groups'), parts along dimension 0
The draws below stay inside these ranges and needn't reach their ends.
There are 2 independent parts, one for each index of `groups`. The reference program is written for one: setup_inputs(seed, part) draws one part's arguments, and reference() takes and returns one part's arrays. A program takes and returns all parts, laid end to end along the dimension named above; an argument that names none is the same for every part. Nothing has to cross between parts.
All inputs are finite; a program needn't handle non-finite values.
Results may differ from the reference program's by a relative error of at most 0.001.
Values sent between devices are 32-bit elements; how exact they have to be, the bound alone decides.
No kernel may reach another device: no remote copies, remote signals or barrier semaphores. Data moves between devices by JAX's collectives and lax.ppermute only.
A program may use at most 64 MiB of HBM per device.

```python
import math
import jax
import jax.numpy as jnp
from jax import lax

H = 256
P_SIZE = 32
N = 128
WALKERS = 8


def place_ends(result, key, low, high):
    shape = result.shape
    place = [jax.random.randint(jax.random.fold_in(key, axis), (), 0, shape[axis]) for axis in range(len(shape))]
    result = result.at[tuple(place)].set(low)
    longest = shape.index(max(shape))
    place[longest] = (place[longest] + 1) % shape[longest]
    return result.at[tuple(place)].set(high)


def block_scale(stream_key, shape, shards, smallest, largest):
    gain = 1.0
    for axis_at, parts in shards:
        steps = jax.random.uniform(jax.random.fold_in(jax.random.fold_in(stream_key, 6), axis_at), (parts,), jnp.float32, smallest / len(shards), largest / len(shards))
        gain = gain * jnp.repeat(jnp.exp(steps), shape[axis_at] // parts).reshape((-1,) + (1,) * (len(shape) - 1 - axis_at))
    return gain


def bell_draw(own_key, shape, spread, limit, cuts=(), kind=jnp.bfloat16):
    values = jax.random.normal(own_key, shape, jnp.float32) * spread
    if len(cuts) > 0:
        values = block_scale(own_key, shape, cuts, -0.22, 0.18) * values
    return jnp.clip(values, min=-limit, max=limit).astype(kind)


def setup_inputs(seed: int = 0, part: int = 0) -> dict:
    splits = jax.random.split(jax.random.key(seed), 10)
    part_keys = jax.random.split(jax.random.fold_in(splits[9], part), 10)
    return {
        "hidden": bell_draw(part_keys[0], (WALKERS, N, H), 1.0, 6.0, ((0, 2), (1, 8))),
        "cotangent": bell_draw(part_keys[1], (WALKERS, N, H), 1.0, 6.0, ((0, 2), (1, 8))),
        "positions": jnp.clip(1.0 * jax.random.uniform(part_keys[2], (WALKERS, 3, N), jnp.float32) ** block_scale(part_keys[2], (WALKERS, 3, N), ((0, 2), (2, 8)), -0.2, 0.2), 0.0, 1.0),
        "spins": place_ends(jax.random.randint(part_keys[3], (N,), 0, 2), jax.random.fold_in(part_keys[3], 1), 0, 1).astype(jnp.int32),
        "w_in": bell_draw(splits[4], (H, P_SIZE), H ** -0.5, 0.375),
        "w_pair": bell_draw(splits[5], (P_SIZE, P_SIZE), P_SIZE ** -0.5, 1.0, (), jnp.float32),
        "spin_bias": bell_draw(splits[6], (2, P_SIZE), 0.5, 3.0, (), jnp.float32),
        "rates": jnp.clip(jnp.exp(jax.random.uniform(splits[7], (P_SIZE,), jnp.float32, math.log(1.0), math.log(100.0))), 1.0, 100.0),
        "w_out": bell_draw(splits[8], (P_SIZE, H), P_SIZE ** -0.5, 1.0),
    }


def walker_grads(hidden_w, cotangent_w, positions_w, spins, w_in, w_pair, spin_bias, rates, w_out):
    highest = lax.Precision.HIGHEST
    count = hidden_w.shape[0]
    projected = jnp.dot(hidden_w, w_in, preferred_element_type=jnp.float32)
    sensitivity = jnp.dot(cotangent_w, w_out.T, preferred_element_type=jnp.float32) / count
    offset = positions_w[:, :, None] - positions_w[:, None, :]
    wrapped = jnp.sin(jnp.pi * offset) / jnp.pi
    squared = jnp.sum(wrapped * wrapped, axis=0)
    radial = jnp.exp(-squared[:, :, None] * rates)
    linear = jnp.einsum("ijp,pq->ijq", radial, w_pair, precision=highest)
    same_spin = (spins[:, None] == spins[None, :]).astype(jnp.float32)[:, :, None]
    bias = same_spin * spin_bias[1] + (1.0 - same_spin) * spin_bias[0]
    activity = jnp.tanh(projected[:, None, :] + projected[None, :, :] + linear + bias)
    keep_mask = (1.0 - jnp.eye(count, dtype=jnp.float32))[:, :, None]
    slope = (1.0 - activity * activity) * keep_mask
    symmetric = (sensitivity[:, None, :] + sensitivity[None, :, :]) * slope
    own_part = sensitivity[:, None, :] * slope
    row_sens = jnp.sum(symmetric, axis=1)
    row_mean = jnp.sum(activity * keep_mask, axis=1)
    hidden_grad = jnp.einsum("ip,hp->ih", row_sens, w_in.astype(jnp.float32), precision=highest).astype(jnp.bfloat16)
    w_in_part = jnp.einsum("ih,ip->hp", hidden_w.astype(jnp.float32), row_sens, precision=highest)
    pair_part = jnp.einsum("ijp,ijq->pq", radial, own_part, precision=highest)
    bias_part = jnp.stack([jnp.sum(own_part * (1.0 - same_spin), axis=(0, 1)), jnp.sum(own_part * same_spin, axis=(0, 1))])
    out_part = jnp.einsum("ip,ih->ph", row_mean, cotangent_w.astype(jnp.float32), precision=highest) / count
    return hidden_grad, w_in_part, pair_part, bias_part, out_part


def reference(hidden, cotangent, positions, spins, w_in, w_pair, spin_bias, rates, w_out):
    def one_walker(items):
        return walker_grads(items[0], items[1], items[2], spins, w_in, w_pair, spin_bias, rates, w_out)

    hidden_grad, w_in_part, pair_part, bias_part, out_part = lax.map(one_walker, (hidden, cotangent, positions))
    return hidden_grad, jnp.sum(w_in_part, axis=0), jnp.sum(pair_part, axis=0), jnp.sum(bias_part, axis=0), jnp.sum(out_part, axis=0)
```

```python
import functools

import jax
import jax.numpy as jnp
from jax import lax
from jax.experimental import pallas as pl
from jax.experimental.pallas import tpu as pltpu
from jax.sharding import PartitionSpec as P


F32, BF16 = jnp.float32, jnp.bfloat16
LANES = 128
PACK = 8


def dot(a, b, dims=((1,), (0,))):
    return lax.dot_general(a, b, (dims, ((), ())), preferred_element_type=F32)


def dot_exact(a, b, dims=((1,), (0,))):
    return lax.dot_general(
        a, b, (dims, ((), ())), precision=lax.Precision.HIGHEST, preferred_element_type=F32
    )


def split(x):
    high = x.astype(BF16)
    return high, (x - high.astype(F32)).astype(BF16)


def iota(shape, axis):
    return lax.broadcasted_iota(jnp.int32, shape, axis)


def flag(condition):
    return jnp.where(condition, 1.0, 0.0).astype(F32)


def embed_kernel(total, hid, cot, pos, spin, w_in, w_out, out):
    walkers, rows, _ = hid.shape
    proj, sense = [], []
    for w in range(walkers):
        proj.append(dot(hid[w], w_in[...]))
        sense.append(dot(cot[w], w_out[...], ((1,), (1,))) / total)
    out[0:rows] = jnp.concatenate(proj, axis=1)
    out[rows : 2 * rows] = jnp.concatenate(sense, axis=1)
    place = iota((8, rows), 0)
    feats = []
    for w in range(walkers):
        x = pos[w]
        turn = jnp.concatenate([x, x - 0.25, jnp.zeros((2, rows), F32)], axis=0)
        feat = jnp.cos(turn * (2.0 * jnp.pi))
        feat = jnp.where(place == 6, jnp.broadcast_to(spin[...].astype(F32), (8, rows)), feat)
        feats.append(jnp.where(place == 7, 1.0, feat))
    feat = jnp.concatenate(feats, axis=0).T
    parts = [feat[8 * k : 8 * k + 8] for k in range(rows // 8)]
    parts.append(jnp.zeros((8, LANES - 8 * walkers * (rows // 8)), F32))
    out[2 * rows : 2 * rows + 8] = jnp.concatenate(parts, axis=1)


def spread(x, w, width):
    lane = iota(x.shape, 1) // width
    x = jnp.where(lane == w, x, 0.0)
    step = width
    while step < LANES:
        x = x + pltpu.roll(x, step, 1)
        step *= 2
    return x


def pair_kernel(total, slots, *refs):
    side = refs[0]
    gathered = refs[1 : 1 + len(slots)]
    hid, cot, w_in, w_pair, spin_bias, rates = refs[1 + len(slots) : 7 + len(slots)]
    grad_out, keep_out, send_out = refs[7 + len(slots) :]
    walkers, rows, hidden_width = hid.shape
    width = w_pair.shape[0]
    block = 2 * rows + 8
    lanes = PACK * width
    feats = 8 * walkers
    pieces = [(ref, block * s) for ref, n in zip(gathered, slots) for s in range(n)]
    proj_all = jnp.concatenate([r[s : s + rows] for r, s in pieces], axis=0)
    sense_all = jnp.concatenate([r[s + rows : s + 2 * rows] for r, s in pieces], axis=0)
    misc = []
    for r, s in pieces:
        packed = r[s + 2 * rows : s + block]
        for k in range(rows // 8):
            misc.append(packed if k == 0 else pltpu.roll(packed, LANES - feats * k, 1))
    misc = jnp.concatenate(misc, axis=0)[:, :feats]
    own_misc = misc[:rows]
    spin_col = jnp.broadcast_to(misc[:, 6:7], (total, LANES))
    sel = flag(iota((lanes, width), 0) % width == iota((lanes, width), 1))
    sel_t = flag(iota((width, lanes), 1) % width == iota((width, lanes), 0))
    same_group = iota((lanes, lanes), 0) // width == iota((lanes, lanes), 1) // width
    sel16, sel_t16 = sel.astype(BF16), sel_t.astype(BF16)
    pair_parts = split(w_pair[...])
    big = [
        jnp.where(same_group, dot(dot(sel16, part).astype(BF16), sel_t16), 0.0).astype(BF16)
        for part in pair_parts
    ]
    rate_row = dot_exact(rates[...], sel_t) * (0.5 / (jnp.pi * jnp.pi))
    bias_rows = dot_exact(spin_bias[...], sel_t)
    bias_low = bias_rows[0:1]
    bias_step = bias_rows[1:2] - bias_rows[0:1]
    own_proj = proj_all[:rows]
    own_sense = sense_all[:rows]
    feat_row = iota((feats, lanes), 0)
    far = jnp.float32(16384.0)
    grams = None
    sens_rows, mean_rows = [], []
    bias_same = jnp.zeros((1, lanes), F32)
    bias_all = jnp.zeros((1, lanes), F32)
    columns = [
        (spread(proj_all, w, width), spread(sense_all, w, width)) for w in range(walkers)
    ]

    def wide(x):
        return jnp.concatenate([x] * (lanes // LANES), axis=1)

    spin_wide = wide(spin_col)
    radial_parts, own_parts = [], []
    for w in range(walkers):
        col_proj, col_sense = wide(columns[w][0]), wide(columns[w][1])
        for h in range(rows // PACK):
            group = flag(iota((rows, lanes), 1) // width + PACK * h == iota((rows, lanes), 0))
            own_cols = dot_exact(own_misc, group, ((0,), (0,)))
            in_walker = (feat_row >= 8 * w) & (feat_row < 8 * w + 6)
            basis = jnp.where(in_walker, own_cols, jnp.where(feat_row == 8 * w + 7, -3.0, 0.0))
            radial = jnp.exp(dot_exact(misc, basis * rate_row))
            row_proj = jnp.sum(wide(columns[w][0][:rows]) * group, axis=0, keepdims=True)
            row_sense = jnp.sum(wide(columns[w][1][:rows]) * group, axis=0, keepdims=True)
            row_spin = own_cols[6:7]
            row_base = row_proj + bias_low + (1.0 - row_spin) * bias_step
            row_turn = (2.0 * row_spin - 1.0) * bias_step
            high, low = split(radial)
            z = dot(high, big[0]) + dot(low, big[0]) + dot(high, big[1])
            z = z + col_proj + (row_base + spin_wide * row_turn)
            z = jnp.concatenate([z[:rows] + group * far, z[rows:]], axis=0)
            m = jnp.tanh(z)
            slope = 1.0 - m * m
            own = slope * row_sense
            sum_slope = jnp.sum(slope, axis=0, keepdims=True)
            sum_spin = jnp.sum(slope * spin_wide, axis=0, keepdims=True)
            sum_col = jnp.sum(slope * col_sense, axis=0, keepdims=True)
            mean_rows.append(jnp.sum(m, axis=0, keepdims=True) - 1.0)
            sens_rows.append(row_sense * sum_slope + sum_col)
            bias_all = bias_all + row_sense * sum_slope
            bias_same = bias_same + row_sense * (
                (1.0 - row_spin) * sum_slope + (2.0 * row_spin - 1.0) * sum_spin
            )
            own_high, own_low = split(own)
            tn = ((0,), (0,))
            gram = dot(high, own_high, tn) + dot(low, own_high, tn) + dot(high, own_low, tn)
            grams = gram if grams is None else grams + gram
    n_tiles = len(sens_rows)
    n_rows = walkers * rows
    stack = jnp.concatenate(
        [jnp.concatenate(sens_rows, axis=0), jnp.concatenate(mean_rows, axis=0)], axis=1
    )
    expand = flag(iota((n_rows, n_tiles), 0) // PACK == iota((n_rows, n_tiles), 1))
    mine = iota((n_rows, lanes), 1) // width == iota((n_rows, lanes), 0) % PACK
    tall = dot_exact(expand, stack)
    row_sens = dot_exact(jnp.where(mine, tall[:, :lanes], 0.0), sel)
    row_mean = dot_exact(jnp.where(mine, tall[:, lanes:], 0.0), sel)
    w_in_wide = w_in[...].astype(F32)
    for w in range(walkers):
        part = row_sens[w * rows : (w + 1) * rows]
        grad_out[w] = dot_exact(part, w_in_wide, ((1,), (1,))).astype(BF16)
    tn = ((0,), (0,))
    hid_all = jnp.concatenate([hid[w].astype(F32) for w in range(walkers)], axis=0)
    cot_all = jnp.concatenate([cot[w].astype(F32) for w in range(walkers)], axis=0)
    in_part = dot_exact(row_sens, hid_all, tn)
    out_part = dot_exact(row_mean, cot_all, tn) / total
    gram = dot_exact(jnp.where(same_group, grams, 0.0), sel)
    pair_part = gram[0:width]
    for a in range(1, PACK):
        pair_part = pair_part + gram[a * width : (a + 1) * width]
    bias_part = dot_exact(
        jnp.concatenate([bias_all - bias_same, bias_same, jnp.zeros((6, lanes), F32)], axis=0), sel
    )
    pair_rows = [pair_part[8 * k : 8 * k + 8] for k in range(width // 8)]
    tail = jnp.concatenate(
        pair_rows + [bias_part, jnp.zeros((8, hidden_width - width * (width // 8 + 1)), F32)],
        axis=1,
    )
    full = jnp.concatenate([in_part, out_part, tail], axis=0)
    half = hidden_width // 2
    first = side[0] == 0
    keep_out[...] = jnp.where(first, full[:, :half], full[:, half:])
    send_out[...] = jnp.where(first, full[:, half:], full[:, :half])


def finish_kernel(side, mine, other, w_in_grad, w_pair_grad, bias_grad, w_out_grad):
    width = w_pair_grad.shape[0]
    first = side[0] == 0
    low = jnp.where(first, mine[...], other[...])
    high = jnp.where(first, other[...], mine[...])
    full = jnp.concatenate([low, high], axis=1)
    w_in_grad[...] = full[:width].T
    w_out_grad[...] = full[width : 2 * width]
    tail = full[2 * width :]
    for k in range(width // 8):
        w_pair_grad[8 * k : 8 * k + 8] = tail[:, k * width : (k + 1) * width]
    at = (width // 8) * width
    bias_grad[...] = tail[0:2, at : at + width]


VMEM = pl.BlockSpec(memory_space=pltpu.VMEM)
SMEM = pl.BlockSpec(memory_space=pltpu.SMEM)


def swap(x, axis, size, mask):
    return lax.ppermute(x, axis, [(i, i ^ mask) for i in range(size)])


def stages(blocks):
    groups, top = [], blocks
    while top > 2:
        groups.append((top // 4, top // 2, 3 * top // 4))
        top //= 4
    if top == 2:
        groups.append((1,))
    return groups


def on_device(hidden, cotangent, positions, spins, w_in, w_pair, spin_bias, rates, w_out):
    blocks = lax.axis_size("elec")
    walkers, rows, hidden_width = hidden.shape
    width = w_in.shape[1]
    total = rows * blocks
    side = lax.axis_index("walk").astype(jnp.int32).reshape(1)
    block = 2 * rows + 8
    payload = pl.pallas_call(
        functools.partial(embed_kernel, total),
        out_shape=jax.ShapeDtypeStruct((block, LANES), F32),
        in_specs=[VMEM] * 6,
        out_specs=VMEM,
        name="embed",
    )(hidden, cotangent, positions, spins.reshape(1, rows), w_in, w_out)
    groups = stages(blocks)
    gathered = [payload]
    for masks in groups:
        whole = gathered[0] if len(gathered) == 1 else jnp.concatenate(gathered, axis=0)
        gathered = [whole] + [swap(whole, "elec", blocks, m) for m in masks]
    slots = tuple(g.shape[0] // block for g in gathered)
    flat = 2 * width + 8
    grad, keep, send = pl.pallas_call(
        functools.partial(pair_kernel, total, slots),
        out_shape=(
            jax.ShapeDtypeStruct(hidden.shape, BF16),
            jax.ShapeDtypeStruct((flat, hidden_width // 2), F32),
            jax.ShapeDtypeStruct((flat, hidden_width // 2), F32),
        ),
        in_specs=[SMEM] + [VMEM] * (len(gathered) + 6),
        out_specs=(VMEM,) * 3,
        name="pairs",
    )(side, *gathered, hidden, cotangent, w_in, w_pair, spin_bias, rates.reshape(1, width))
    mine = keep + swap(send, "walk", 2, 1)
    for masks in reversed(groups):
        got = [swap(mine, "elec", blocks, m) for m in masks]
        mine = mine + got[0]
        if len(got) == 3:
            mine = mine + (got[1] + got[2])
    other = swap(mine, "walk", 2, 1)
    w_in_grad, w_pair_grad, spin_bias_grad, w_out_grad = pl.pallas_call(
        finish_kernel,
        out_shape=(
            jax.ShapeDtypeStruct((hidden_width, width), F32),
            jax.ShapeDtypeStruct((width, width), F32),
            jax.ShapeDtypeStruct((2, width), F32),
            jax.ShapeDtypeStruct((width, hidden_width), F32),
        ),
        in_specs=[SMEM, VMEM, VMEM],
        out_specs=(VMEM,) * 4,
        name="finish",
    )(side, mine, other)
    return (grad, w_in_grad, w_pair_grad, spin_bias_grad, w_out_grad)


def solution(mesh):
    return jax.shard_map(
        on_device,
        mesh=mesh,
        in_specs=(
            P(("groups", "walk"), "elec", None),
            P(("groups", "walk"), "elec", None),
            P(("groups", "walk"), None, "elec"),
            P(("groups", "elec")),
            P(),
            P(),
            P(),
            P(),
            P(),
        ),
        out_specs=(
            P(("groups", "walk"), "elec", None),
            P("groups", None),
            P("groups", None),
            P("groups", None),
            P("groups", None),
        ),
        check_vma=False,
    )
```

```python
import functools

import jax
import jax.numpy as jnp
from jax import lax
from jax.experimental import pallas as pl
from jax.experimental.pallas import tpu as pltpu
from jax.sharding import PartitionSpec as P


F32, BF16 = jnp.float32, jnp.bfloat16
LANES = 128
PACK = 8


def dot(a, b, dims=((1,), (0,))):
    return lax.dot_general(a, b, (dims, ((), ())), preferred_element_type=F32)


def dot_exact(a, b, dims=((1,), (0,))):
    return lax.dot_general(
        a, b, (dims, ((), ())), precision=lax.Precision.HIGHEST, preferred_element_type=F32
    )


def split(x):
    high = x.astype(BF16)
    return high, (x - high.astype(F32)).astype(BF16)


def iota(shape, axis):
    return lax.broadcasted_iota(jnp.int32, shape, axis)


def flag(condition):
    return jnp.where(condition, 1.0, 0.0).astype(F32)


def embed_kernel(total, hid, cot, pos, spin, w_in, w_out, out):
    walkers, rows, _ = hid.shape
    proj, sense = [], []
    for w in range(walkers):
        proj.append(dot(hid[w], w_in[...], ((1,), (1,))))
        sense.append(dot(cot[w], w_out[...], ((1,), (1,))) / total)
    out[0:rows] = jnp.concatenate(proj, axis=1)
    out[rows : 2 * rows] = jnp.concatenate(sense, axis=1)
    feats = []
    for c in range(3):
        x = pos[c]
        feats.append(jnp.cos(jnp.concatenate([x, x - 0.25], axis=0) * (2.0 * jnp.pi)))
    labels = jnp.broadcast_to(spin[...].astype(F32), (8, rows))
    feats.append(jnp.where(iota((8, rows), 0) == 0, labels, 1.0))
    feat = jnp.concatenate(feats, axis=0).T
    parts = [feat[8 * k : 8 * k + 8] for k in range(rows // 8)]
    parts.append(jnp.zeros((8, LANES - feat.shape[1] * (rows // 8)), F32))
    out[2 * rows : 2 * rows + 8] = jnp.concatenate(parts, axis=1)


def spread(x, w, width):
    lane = iota(x.shape, 1) // width
    x = jnp.where(lane == w, x, 0.0)
    step = width
    while step < LANES:
        x = x + pltpu.roll(x, step, 1)
        step *= 2
    return x


def pair_kernel(total, slots, *refs):
    side = refs[0]
    gathered = refs[1 : 1 + len(slots)]
    hid, cot, w_in, w_pair, spin_bias, rates = refs[1 + len(slots) : 7 + len(slots)]
    grad_out, keep_out, send_out = refs[7 + len(slots) :]
    walkers, rows, hidden_width = hid.shape
    width = w_pair.shape[0]
    block = 2 * rows + 8
    lanes = PACK * width
    feats = 6 * walkers + 8
    spin_at = 6 * walkers
    pieces = [(ref, block * s) for ref, n in zip(gathered, slots) for s in range(n)]
    proj_all = jnp.concatenate([r[s : s + rows] for r, s in pieces], axis=0)
    sense_all = jnp.concatenate([r[s + rows : s + 2 * rows] for r, s in pieces], axis=0)
    misc = []
    for r, s in pieces:
        packed = r[s + 2 * rows : s + block]
        for k in range(rows // 8):
            misc.append(packed if k == 0 else pltpu.roll(packed, LANES - feats * k, 1))
    misc = jnp.concatenate(misc, axis=0)[:, :feats]
    own_misc = misc[:rows]
    spin_col = jnp.broadcast_to(misc[:, spin_at : spin_at + 1], (total, LANES))
    sel = flag(iota((lanes, width), 0) % width == iota((lanes, width), 1))
    sel_t = flag(iota((width, lanes), 1) % width == iota((width, lanes), 0))
    same_group = iota((lanes, lanes), 0) // width == iota((lanes, lanes), 1) // width
    sel16, sel_t16 = sel.astype(BF16), sel_t.astype(BF16)
    pair_parts = split(w_pair[...])
    big = [
        jnp.where(same_group, dot(dot(sel16, part).astype(BF16), sel_t16), 0.0).astype(BF16)
        for part in pair_parts
    ]
    rate_row = dot_exact(rates[...], sel_t) * (0.5 / (jnp.pi * jnp.pi))
    bias_rows = dot_exact(spin_bias[...], sel_t)
    bias_low = bias_rows[0:1]
    bias_step = bias_rows[1:2] - bias_rows[0:1]
    own_proj = proj_all[:rows]
    own_sense = sense_all[:rows]
    feat_row = iota((feats, lanes), 0)
    far = jnp.float32(16384.0)
    grams = None
    sens_rows, mean_rows = [], []
    bias_same = jnp.zeros((1, lanes), F32)
    bias_all = jnp.zeros((1, lanes), F32)
    columns = [
        (spread(proj_all, w, width), spread(sense_all, w, width)) for w in range(walkers)
    ]

    def wide(x):
        return jnp.concatenate([x] * (lanes // LANES), axis=1)

    spin_wide = wide(spin_col)
    radial_parts, own_parts = [], []
    for w in range(walkers):
        col_proj, col_sense = wide(columns[w][0]), wide(columns[w][1])
        for h in range(rows // PACK):
            group = flag(iota((rows, lanes), 1) // width + PACK * h == iota((rows, lanes), 0))
            own_cols = dot_exact(own_misc, group, ((0,), (0,)))
            in_walker = (feat_row < spin_at) & (feat_row % walkers == w)
            basis = jnp.where(in_walker, own_cols, jnp.where(feat_row == spin_at + 1, -3.0, 0.0))
            radial = jnp.exp(dot_exact(misc, basis * rate_row))
            row_proj = jnp.sum(wide(columns[w][0][:rows]) * group, axis=0, keepdims=True)
            row_sense = jnp.sum(wide(columns[w][1][:rows]) * group, axis=0, keepdims=True)
            row_spin = own_cols[spin_at : spin_at + 1]
            row_base = row_proj + bias_low + (1.0 - row_spin) * bias_step
            row_turn = (2.0 * row_spin - 1.0) * bias_step
            high, low = split(radial)
            z = dot(high, big[0]) + dot(low, big[0]) + dot(high, big[1])
            z = z + col_proj + (row_base + spin_wide * row_turn)
            z = jnp.concatenate([z[:rows] + group * far, z[rows:]], axis=0)
            m = jnp.tanh(z)
            slope = 1.0 - m * m
            own = slope * row_sense
            sum_slope = jnp.sum(slope, axis=0, keepdims=True)
            sum_spin = jnp.sum(slope * spin_wide, axis=0, keepdims=True)
            sum_col = jnp.sum(slope * col_sense, axis=0, keepdims=True)
            mean_rows.append(jnp.sum(m, axis=0, keepdims=True) - 1.0)
            sens_rows.append(row_sense * sum_slope + sum_col)
            bias_all = bias_all + row_sense * sum_slope
            bias_same = bias_same + row_sense * (
                (1.0 - row_spin) * sum_slope + (2.0 * row_spin - 1.0) * sum_spin
            )
            own_high, own_low = split(own)
            tn = ((0,), (0,))
            gram = dot(high, own_high, tn) + dot(low, own_high, tn) + dot(high, own_low, tn)
            grams = gram if grams is None else grams + gram
    n_tiles = len(sens_rows)
    n_rows = walkers * rows
    stack = jnp.concatenate(
        [jnp.concatenate(sens_rows, axis=0), jnp.concatenate(mean_rows, axis=0)], axis=1
    )
    expand = flag(iota((n_rows, n_tiles), 0) // PACK == iota((n_rows, n_tiles), 1))
    mine = iota((n_rows, lanes), 1) // width == iota((n_rows, lanes), 0) % PACK
    tall = dot_exact(expand, stack)
    row_sens = dot_exact(jnp.where(mine, tall[:, :lanes], 0.0), sel)
    row_mean = dot_exact(jnp.where(mine, tall[:, lanes:], 0.0), sel)
    w_in_wide = w_in[...].astype(F32)
    for w in range(walkers):
        part = row_sens[w * rows : (w + 1) * rows]
        grad_out[w] = dot_exact(part, w_in_wide).astype(BF16)
    tn = ((0,), (0,))
    hid_all = jnp.concatenate([hid[w].astype(F32) for w in range(walkers)], axis=0)
    cot_all = jnp.concatenate([cot[w].astype(F32) for w in range(walkers)], axis=0)
    in_part = dot_exact(row_sens, hid_all, tn)
    out_part = dot_exact(row_mean, cot_all, tn) / total
    gram = dot_exact(jnp.where(same_group, grams, 0.0), sel)
    pair_part = gram[0:width]
    for a in range(1, PACK):
        pair_part = pair_part + gram[a * width : (a + 1) * width]
    bias_part = dot_exact(
        jnp.concatenate([bias_all - bias_same, bias_same, jnp.zeros((6, lanes), F32)], axis=0), sel
    )
    pair_rows = [pair_part[8 * k : 8 * k + 8] for k in range(width // 8)]
    tail = jnp.concatenate(
        pair_rows + [bias_part, jnp.zeros((8, hidden_width - width * (width // 8 + 1)), F32)],
        axis=1,
    )
    full = jnp.concatenate([in_part, out_part, tail], axis=0)
    half = hidden_width // 2
    first = side[0] == 0
    keep_out[...] = jnp.where(first, full[:, :half], full[:, half:])
    send_out[...] = jnp.where(first, full[:, half:], full[:, :half])


def finish_kernel(side, mine, other, w_in_grad, w_pair_grad, bias_grad, w_out_grad):
    width = w_pair_grad.shape[0]
    first = side[0] == 0
    low = jnp.where(first, mine[...], other[...])
    high = jnp.where(first, other[...], mine[...])
    full = jnp.concatenate([low, high], axis=1)
    w_in_grad[...] = full[:width]
    w_out_grad[...] = full[width : 2 * width]
    tail = full[2 * width :]
    for k in range(width // 8):
        w_pair_grad[8 * k : 8 * k + 8] = tail[:, k * width : (k + 1) * width]
    at = (width // 8) * width
    bias_grad[...] = tail[0:2, at : at + width]


VMEM = pl.BlockSpec(memory_space=pltpu.VMEM)
SMEM = pl.BlockSpec(memory_space=pltpu.SMEM)


def near(x):
    return pltpu.with_memory_space_constraint(x, pltpu.VMEM)


def swap(x, axis, size, mask):
    return lax.ppermute(x, axis, [(i, i ^ mask) for i in range(size)])


def stages(blocks):
    groups, top = [], blocks
    while top > 2:
        groups.append((top // 4, top // 2, 3 * top // 4))
        top //= 4
    if top == 2:
        groups.append((1,))
    return groups


def on_device(hidden, cotangent, positions, spins, w_in, w_pair, spin_bias, rates, w_out):
    blocks = lax.axis_size("elec")
    walkers, rows, hidden_width = hidden.shape
    width = w_in.shape[1]
    total = rows * blocks
    side = lax.axis_index("walk").astype(jnp.int32).reshape(1)
    block = 2 * rows + 8
    payload = pl.pallas_call(
        functools.partial(embed_kernel, total),
        out_shape=pltpu.VMEM((block, LANES), F32),
        in_specs=[VMEM] * 6,
        out_specs=VMEM,
        name="embed",
    )(hidden, cotangent, positions.transpose(1, 0, 2), spins.reshape(1, rows), w_in.T, w_out)
    groups = stages(blocks)
    gathered = [payload]
    for masks in groups:
        whole = gathered[0] if len(gathered) == 1 else jnp.concatenate(gathered, axis=0)
        gathered = [whole] + [swap(whole, "elec", blocks, m) for m in masks]
    slots = tuple(g.shape[0] // block for g in gathered)
    flat = 2 * width + 8
    grad, keep, send = pl.pallas_call(
        functools.partial(pair_kernel, total, slots),
        out_shape=(
            jax.ShapeDtypeStruct(hidden.shape, BF16),
            pltpu.VMEM((flat, hidden_width // 2), F32),
            pltpu.VMEM((flat, hidden_width // 2), F32),
        ),
        in_specs=[SMEM] + [VMEM] * (len(gathered) + 6),
        out_specs=(VMEM,) * 3,
        name="pairs",
    )(side, *[near(g) for g in gathered], hidden, cotangent, w_in.T, w_pair, spin_bias, rates.reshape(1, width))
    mine = keep + swap(send, "walk", 2, 1)
    for masks in reversed(groups):
        got = [swap(mine, "elec", blocks, m) for m in masks]
        mine = mine + got[0]
        if len(got) == 3:
            mine = mine + (got[1] + got[2])
    other = swap(mine, "walk", 2, 1)
    w_in_grad, w_pair_grad, spin_bias_grad, w_out_grad = pl.pallas_call(
        finish_kernel,
        out_shape=(
            jax.ShapeDtypeStruct((width, hidden_width), F32),
            jax.ShapeDtypeStruct((width, width), F32),
            jax.ShapeDtypeStruct((2, width), F32),
            jax.ShapeDtypeStruct((width, hidden_width), F32),
        ),
        in_specs=[SMEM, VMEM, VMEM],
        out_specs=(VMEM,) * 4,
        name="finish",
    )(side, near(mine), near(other))
    return (grad, w_in_grad.T, w_pair_grad, spin_bias_grad, w_out_grad)


def solution(mesh):
    return jax.shard_map(
        on_device,
        mesh=mesh,
        in_specs=(
            P(("groups", "walk"), "elec", None),
            P(("groups", "walk"), "elec", None),
            P(("groups", "walk"), None, "elec"),
            P(("groups", "elec")),
            P(),
            P(),
            P(),
            P(),
            P(),
        ),
        out_specs=(
            P(("groups", "walk"), "elec", None),
            P("groups", None),
            P("groups", None),
            P("groups", None),
            P("groups", None),
        ),
        check_vma=False,
    )
```

```python
import functools

import jax
import jax.numpy as jnp
from jax import lax
from jax.experimental import pallas as pl
from jax.experimental.pallas import tpu as pltpu
from jax.sharding import PartitionSpec as P


F32, BF16 = jnp.float32, jnp.bfloat16
LANES = 128
PACK = 8


def dot(a, b, dims=((1,), (0,))):
    return lax.dot_general(a, b, (dims, ((), ())), preferred_element_type=F32)


def dot_exact(a, b, dims=((1,), (0,))):
    return lax.dot_general(
        a, b, (dims, ((), ())), precision=lax.Precision.HIGHEST, preferred_element_type=F32
    )


def split(x):
    high = x.astype(BF16)
    return high, (x - high.astype(F32)).astype(BF16)


def iota(shape, axis):
    return lax.broadcasted_iota(jnp.int32, shape, axis)


def flag(condition):
    return jnp.where(condition, 1.0, 0.0).astype(F32)


def embed_kernel(total, hid, cot, pos, spin, w_in, w_out, w_pair, spin_bias, rates, out, big_out, *copies):
    walkers, rows, hidden_width = hid.shape
    proj, sense = [], []
    block = 2 * rows + 8
    n_rows = walkers * rows
    for w in range(walkers):
        proj.append(dot(hid[w], w_in[...], ((1,), (1,))))
        sense.append(dot(cot[w], w_out[...], ((1,), (1,))) / total)
        for k in range(hidden_width // LANES):
            at = block + k * n_rows + w * rows
            big_out[at : at + rows] = hid[w][:, k * LANES : (k + 1) * LANES].astype(F32)
            at = at + hidden_width // LANES * n_rows
            big_out[at : at + rows] = cot[w][:, k * LANES : (k + 1) * LANES].astype(F32)
    feats = []
    for c in range(3):
        x = pos[c]
        feats.append(jnp.cos(jnp.concatenate([x, x - 0.25], axis=0) * (2.0 * jnp.pi)))
    labels = jnp.broadcast_to(spin[...].astype(F32), (8, rows))
    feats.append(jnp.where(iota((8, rows), 0) == 0, labels, 1.0))
    feat = jnp.concatenate(feats, axis=0).T
    parts = [feat[8 * k : 8 * k + 8] for k in range(rows // 8)]
    parts.append(jnp.zeros((8, LANES - feat.shape[1] * (rows // 8)), F32))
    mine = jnp.concatenate(
        [
            jnp.concatenate(proj, axis=1),
            jnp.concatenate(sense, axis=1),
            jnp.concatenate(parts, axis=1),
        ],
        axis=0,
    )
    out[...] = mine
    big_out[0:block] = mine
    for ref, copy in zip((w_in, w_pair, spin_bias, rates), copies):
        copy[...] = ref[...]


def ripple(x, width):
    step = width
    while step < LANES:
        x = x + pltpu.roll(x, step, 1)
        step *= 2
    return x


def spread(x, w, width):
    return ripple(jnp.where(iota(x.shape, 1) // width == w, x, 0.0), width)


def wide(x):
    return jnp.concatenate([x, x], axis=1)


def thirds(x):
    high = x.astype(BF16)
    rest = x - high.astype(F32)
    middle = rest.astype(BF16)
    return high, middle, (rest - middle.astype(F32)).astype(BF16)


def features(packed, rows, feats):
    parts = [packed] + [pltpu.roll(packed, LANES - feats * k, 1) for k in range(1, rows // 8)]
    return jnp.concatenate(parts, axis=0)


def prepare_kernel(walkers, rows, own, w_pair, spin_bias, rates, basis_out, rows_out, *mix_out):
    width = w_pair.shape[0]
    lanes = PACK * width
    spin_at = 6 * walkers
    feats = spin_at + 8
    if mix_out:
        sel = flag(iota((LANES, width), 0) % width == iota((LANES, width), 1)).astype(BF16)
        sel_t = flag(iota((width, LANES), 1) % width == iota((width, LANES), 0)).astype(BF16)
        same = iota((LANES, LANES), 0) // width == iota((LANES, LANES), 1) // width
        high, low = [
            jnp.where(same, dot(dot(sel, part).astype(BF16), sel_t), 0.0) for part in split(w_pair[...])
        ]
        top = jnp.concatenate([high, low], axis=1)
        bottom = jnp.concatenate([high, jnp.zeros_like(high)], axis=1)
        mix_out[0][...] = jnp.concatenate([top, bottom], axis=0).astype(BF16)
    sel_wide = flag(iota((width, lanes), 1) % width == iota((width, lanes), 0))
    rate_row = dot_exact(rates[...], sel_wide) * (0.5 / (jnp.pi * jnp.pi))
    bias_rows = dot_exact(spin_bias[...], sel_wide)
    bias_low, bias_step = bias_rows[0:1], bias_rows[1:2] - bias_rows[0:1]
    proj, sense = own[0:rows], own[rows : 2 * rows]
    feat = features(own[2 * rows : 2 * rows + 8], rows, feats)[:, :feats]
    feat_row = iota((feats, lanes), 0)
    tile = 0
    columns = [(wide(spread(proj, w, width)), wide(spread(sense, w, width))) for w in range(walkers)]
    groups, parts, spins = [], [], []
    for h in range(rows // PACK):
        group = flag(iota((rows, lanes), 1) // width + PACK * h == iota((rows, lanes), 0))
        cols = dot_exact(feat, group, ((0,), (0,)))
        spins.append(cols[spin_at : spin_at + 1])
        groups.append(group)
        parts.append(thirds(jnp.where(feat_row == spin_at + 1, -3.0, cols) * rate_row))
    for w in range(walkers):
        keep = ((feat_row < spin_at) & (feat_row % walkers == w)) | (feat_row == spin_at + 1)
        for h in range(rows // PACK):
            high, middle, low = [jnp.where(keep, p.astype(F32), 0.0).astype(BF16) for p in parts[h]]
            basis_out[:, tile * lanes : (tile + 1) * lanes] = jnp.concatenate(
                [high, middle, low, high, middle, high], axis=0
            )
            row_proj = jnp.sum(columns[w][0] * groups[h], axis=0, keepdims=True)
            row_sense = jnp.sum(columns[w][1] * groups[h], axis=0, keepdims=True)
            rows_out[8 * tile : 8 * tile + 8] = jnp.concatenate(
                [
                    row_sense,
                    row_proj + bias_low + (1.0 - spins[h]) * bias_step,
                    (2.0 * spins[h] - 1.0) * bias_step,
                    spins[h],
                    jnp.zeros((4, lanes), F32),
                ],
                axis=0,
            )
            tile += 1


def fold(x):
    return jnp.sum(x.reshape(x.shape[0] // 8, 8, x.shape[1]), axis=0)


def pair_kernel(walkers, width, rows, total, sets, *refs):
    side, gathered = refs[0], refs[1]
    bigs = refs[2 : 2 + sets]
    bases = refs[2 + sets : 2 + 2 * sets]
    row_sets = refs[2 + 2 * sets : 2 + 3 * sets]
    mix = refs[2 + 3 * sets]
    sens_out, keep_out, send_out, lhs, rhs = refs[3 + 3 * sets :]
    spin_at = 6 * walkers
    feats = spin_at + 8
    lanes = PACK * width
    per_walker = rows // PACK
    tiles = walkers * per_walker
    block = 2 * rows + 8
    starts = [block * s for s in range(gathered.shape[0] // block)]
    proj = jnp.concatenate([gathered[s : s + rows] for s in starts], axis=0)
    sense = jnp.concatenate([gathered[s + rows : s + 2 * rows] for s in starts], axis=0)
    feat = jnp.concatenate(
        [features(gathered[s + 2 * rows : s + block], rows, feats) for s in starts], axis=0
    )
    count = feat.shape[0]
    spin = jnp.broadcast_to(feat[:, spin_at : spin_at + 1], (count, LANES))
    feat = jnp.where(iota(feat.shape, 1) < feats, feat, 0.0)
    high, middle, low = [p.astype(F32) for p in thirds(feat)]
    first = high + pltpu.roll(high, feats, 1) + pltpu.roll(high, 2 * feats, 1)
    first = first + pltpu.roll(middle, 3 * feats, 1)
    second = middle + pltpu.roll(low, feats, 1)
    left = jnp.concatenate([first, second[:, : 2 * feats]], axis=1).astype(BF16)
    halves = [slice(0, LANES), slice(LANES, lanes)]
    group = 2 * count * per_walker
    sums = [[None] * tiles for _ in range(sets)]
    for w in range(walkers):
        col_proj, col_sense = spread(proj, w, width), spread(sense, w, width)
        for n in range(sets):
            base = (w * sets + n) * group
            for k in range(per_walker):
                tile = w * per_walker + k
                radial = jnp.exp(dot(left, bases[n][:, tile * lanes : (tile + 1) * lanes]))
                for i, half in enumerate(halves):
                    at = base + (2 * k + i) * count
                    high, low = split(radial[:, half])
                    lhs[at : at + count] = jnp.concatenate([high, low], axis=1)
            mixed = dot(lhs[base : base + group], mix[...])
            mixed = mixed[:, :LANES] + mixed[:, LANES:]
            for k in range(per_walker):
                tile = w * per_walker + k
                acc = []
                for i, half in enumerate(halves):
                    at = (2 * k + i) * count
                    row_sense = row_sets[n][8 * tile : 8 * tile + 1, half]
                    row_base = row_sets[n][8 * tile + 1 : 8 * tile + 2, half]
                    row_turn = row_sets[n][8 * tile + 2 : 8 * tile + 3, half]
                    z = mixed[at : at + count] + col_proj + (row_base + spin * row_turn)
                    if n == 0:
                        lane = iota((rows, LANES), 1) // width + PACK * k + i * (LANES // width)
                        far = jnp.where(lane == iota((rows, LANES), 0), 16384.0, 0.0)
                        z = jnp.concatenate([z[:rows] + far, z[rows:]], axis=0)
                    m = jnp.tanh(z)
                    slope = 1.0 - m * m
                    high, low = split(slope * row_sense)
                    rhs[base + at : base + at + count] = jnp.concatenate([high, low], axis=1)
                    acc.append((fold(slope), fold(slope * spin), fold(slope * col_sense), fold(m)))
                sums[n][tile] = [jnp.concatenate([a, b], axis=1) for a, b in zip(*acc)]
    tn = ((0,), (0,))
    grams = dot(lhs[...], rhs[...], tn)
    lane8 = iota((8, lanes), 1) // width == iota((8, lanes), 0)
    lane = iota((8, LANES), 1) // width
    sens, mean = [], []
    same_row = jnp.zeros((1, lanes), F32)
    all_row = jnp.zeros((1, lanes), F32)

    def column(row):
        row = jnp.where(lane8, jnp.broadcast_to(row, (8, lanes)), 0.0)
        return ripple(row[:, :LANES] + row[:, LANES:], width)

    for n in range(sets):
        for t in range(tiles):
            slope, turn, col, act = [jnp.sum(x, axis=0, keepdims=True) for x in sums[n][t]]
            row_sense = row_sets[n][8 * t : 8 * t + 1]
            row_spin = row_sets[n][8 * t + 3 : 8 * t + 4]
            own = row_sense * slope
            sens.append(column(own + col))
            mean.append(column(act - 1.0 if n == 0 else act))
            all_row = all_row + own
            same_row = same_row + (1.0 - row_spin) * own
            same_row = same_row + (2.0 * row_spin - 1.0) * (row_sense * turn)
    sens = jnp.concatenate(sens, axis=0)
    mean = jnp.concatenate(mean, axis=0)
    n_rows = walkers * rows
    sens_out[...] = sens[:n_rows]
    lane_all = iota(sens.shape, 1) // width
    both = jnp.where(lane_all == 0, sens, jnp.where(lane_all == 1, mean, 0.0))
    high, low = split(both)
    chunks = (bigs[0].shape[0] - block) // n_rows
    inputs = [
        jnp.concatenate(
            [b[block + k * n_rows : block + (k + 1) * n_rows] for k in range(chunks)], axis=1
        )
        for b in bigs
    ]
    inputs = jnp.concatenate(inputs, axis=0).astype(BF16)
    weights = dot(high, inputs, tn) + dot(low, inputs, tn)
    hidden_width = inputs.shape[1] // 2
    in_part = weights[:width, :hidden_width]
    out_part = weights[width : 2 * width, hidden_width:] / total
    quad = grams[:LANES, :LANES] + grams[LANES:, :LANES] + (grams[:LANES, LANES:] + grams[LANES:, LANES:])
    pair = quad[0:width]
    for k in range(1, LANES // width):
        pair = pair + pltpu.roll(quad[k * width : (k + 1) * width], LANES - k * width, 1)
    tail = jnp.where(lane == 0, pair[0:8], 0.0)
    for k in range(1, width // 8):
        tail = tail + jnp.where(lane == k, pltpu.roll(pair[8 * k : 8 * k + 8], k * width, 1), 0.0)
    pick = iota((8, lanes), 0)
    bias = jnp.where(
        pick == 0,
        jnp.broadcast_to(all_row - same_row, (8, lanes)),
        jnp.where(pick == 1, jnp.broadcast_to(same_row, (8, lanes)), 0.0),
    )
    bias = ripple(bias[:, :LANES] + bias[:, LANES:], width)
    half = hidden_width // 2
    low_half = jnp.concatenate([in_part[:, :half], out_part[:, :half], tail], axis=0)
    high_half = jnp.concatenate([in_part[:, half:], out_part[:, half:], bias], axis=0)
    first = side[0] == 0
    flat = low_half.shape[0]
    keep_out[0:flat] = jnp.where(first, low_half, high_half)
    send_out[0:flat] = jnp.where(first, high_half, low_half)
    place = iota((rows, LANES), 1) // width
    for n in range(1, sets):
        packed = jnp.zeros((rows, LANES), F32)
        for w in range(walkers):
            part = sens[n * n_rows + w * rows : n * n_rows + (w + 1) * rows]
            packed = packed + jnp.where(place == w, part, 0.0)
        at = flat + (n - 1) * rows
        keep_out[at : at + rows] = packed
        send_out[at : at + rows] = jnp.zeros((rows, LANES), F32)


def hidden_kernel(offsets, sens, w_in, *refs):
    received, grad_out = refs[:-1], refs[-1]
    walkers, rows, _ = grad_out.shape
    width = w_in.shape[0]
    total = []
    for w in range(walkers):
        part = sens[w * rows : (w + 1) * rows]
        for at, ref in zip(offsets, received):
            part = part + spread(ref[at : at + rows], w, width)
        total.append(part)
    high, low = split(jnp.concatenate(total, axis=0))
    both = jnp.concatenate([high[:, :width], low[:, :width]], axis=1)
    grad = dot(both, jnp.concatenate([w_in[...], w_in[...]], axis=0))
    for w in range(walkers):
        grad_out[w] = grad[w * rows : (w + 1) * rows].astype(BF16)


def finish_kernel(side, mine, other, w_in_grad, w_pair_grad, bias_grad, w_out_grad):
    width = w_pair_grad.shape[0]
    first = side[0] == 0
    low = jnp.where(first, mine[...], other[...])
    high = jnp.where(first, other[...], mine[...])
    full = jnp.concatenate([low, high], axis=1)
    w_in_grad[...] = full[:width]
    w_out_grad[...] = full[width : 2 * width]
    tail = full[2 * width :]
    for k in range(width // 8):
        w_pair_grad[8 * k : 8 * k + 8] = tail[:, k * width : (k + 1) * width]
    at = (width // 8) * width
    bias_grad[...] = tail[0:2, at : at + width]


VMEM = pl.BlockSpec(memory_space=pltpu.VMEM)
SMEM = pl.BlockSpec(memory_space=pltpu.SMEM)


def near(x):
    return pltpu.with_memory_space_constraint(x, pltpu.VMEM)


def swap(x, axis, size, mask):
    return lax.ppermute(x, axis, [(i, i ^ mask) for i in range(size)])


def stages(blocks):
    groups, top = [], blocks
    while top > 2:
        groups.append((top // 4, top // 2, 3 * top // 4))
        top //= 4
    if top == 2:
        groups.append((1,))
    return groups


def join(mine, got):
    mine = mine + got[0]
    return mine + (got[1] + got[2]) if len(got) == 3 else mine


def on_device(hidden, cotangent, positions, spins, w_in, w_pair, spin_bias, rates, w_out):
    blocks = lax.axis_size("elec")
    walkers, rows, hidden_width = hidden.shape
    width = w_in.shape[1]
    total = rows * blocks
    side = lax.axis_index("walk").astype(jnp.int32).reshape(1)
    block = 2 * rows + 8
    n_rows = walkers * rows
    lanes = PACK * width
    tiles = n_rows // PACK
    groups = stages(blocks)
    col_groups, row_masks = groups[:-1], groups[-1]
    sets = 1 + len(row_masks)
    payload, big, *params = pl.pallas_call(
        functools.partial(embed_kernel, total),
        out_shape=(
            pltpu.VMEM((block, LANES), F32),
            pltpu.VMEM((block + n_rows * 2 * hidden_width // LANES, LANES), F32),
            pltpu.VMEM((width, hidden_width), BF16),
            pltpu.VMEM((width, width), F32),
            pltpu.VMEM((2, width), F32),
            pltpu.VMEM((1, width), F32),
        ),
        in_specs=[VMEM] * 9,
        out_specs=(VMEM,) * 6,
        name="embed",
    )(
        hidden,
        cotangent,
        positions.transpose(1, 0, 2),
        spins.reshape(1, rows),
        w_in.T,
        w_out,
        w_pair,
        spin_bias,
        rates.reshape(1, width),
    )
    w_in_near, *params = [near(p) for p in params]
    bigs = [big] + [swap(big, "elec", blocks, m) for m in row_masks]
    gathered = [payload]
    for masks in col_groups:
        whole = gathered[0] if len(gathered) == 1 else jnp.concatenate(gathered, axis=0)
        gathered = [whole] + [swap(whole, "elec", blocks, m) for m in masks]
    columns = gathered[0] if len(gathered) == 1 else jnp.concatenate(gathered, axis=0)
    depth = 6 * (6 * walkers + 8)

    def prepare(source, first):
        extra = (pltpu.VMEM((lanes, lanes), BF16),) if first else ()
        return pl.pallas_call(
            functools.partial(prepare_kernel, walkers, rows),
            out_shape=(
                pltpu.VMEM((depth, tiles * lanes), BF16),
                pltpu.VMEM((8 * tiles, lanes), F32),
            )
            + extra,
            in_specs=[VMEM] * 4,
            out_specs=(VMEM,) * (2 + len(extra)),
            name="prepare_own" if first else "prepare_row",
        )(near(source), *params)

    basis, row_terms, mix = prepare(payload, True)
    bases, row_sets = [basis], [row_terms]
    for source in bigs[1:]:
        basis, row_terms = prepare(source, False)
        bases.append(basis)
        row_sets.append(row_terms)
    flat = 2 * width + 8
    tall = flat + (sets - 1) * rows
    depth = columns.shape[0] // block * rows * 2 * tiles * sets
    operands = [columns, *bigs, *bases, *row_sets, mix]
    sens, keep, send = pl.pallas_call(
        functools.partial(pair_kernel, walkers, width, rows, total, sets),
        out_shape=(
            pltpu.VMEM((n_rows, LANES), F32),
            pltpu.VMEM((tall, LANES), F32),
            pltpu.VMEM((tall, LANES), F32),
        ),
        in_specs=[SMEM] + [VMEM] * len(operands),
        out_specs=(VMEM,) * 3,
        scratch_shapes=[pltpu.VMEM((depth, 2 * LANES), BF16)] * 2,
        name="pairs",
    )(side, *[near(x) for x in operands])
    mine = keep + swap(send, "walk", 2, 1)
    got = [swap(mine, "elec", blocks, m) for m in row_masks]
    offsets = tuple(flat + n * rows for n in range(len(got)))
    grad = pl.pallas_call(
        functools.partial(hidden_kernel, offsets),
        out_shape=jax.ShapeDtypeStruct(hidden.shape, BF16),
        in_specs=[VMEM] * (2 + len(got)),
        out_specs=VMEM,
        name="hidden_grad",
    )(near(sens), w_in_near, *[near(g) for g in got])
    mine = join(mine[:flat], [g[:flat] for g in got])
    for masks in reversed(col_groups):
        got = [swap(mine, "elec", blocks, m) for m in masks]
        mine = join(mine, got)
    other = swap(mine, "walk", 2, 1)
    w_in_grad, w_pair_grad, spin_bias_grad, w_out_grad = pl.pallas_call(
        finish_kernel,
        out_shape=(
            jax.ShapeDtypeStruct((width, hidden_width), F32),
            jax.ShapeDtypeStruct((width, width), F32),
            jax.ShapeDtypeStruct((2, width), F32),
            jax.ShapeDtypeStruct((width, hidden_width), F32),
        ),
        in_specs=[SMEM, VMEM, VMEM],
        out_specs=(VMEM,) * 4,
        name="finish",
    )(side, near(mine), near(other))
    return (grad, w_in_grad.T, w_pair_grad, spin_bias_grad, w_out_grad)


def solution(mesh):
    return jax.shard_map(
        on_device,
        mesh=mesh,
        in_specs=(
            P(("groups", "walk"), "elec", None),
            P(("groups", "walk"), "elec", None),
            P(("groups", "walk"), None, "elec"),
            P(("groups", "elec")),
            P(),
            P(),
            P(),
            P(),
            P(),
        ),
        out_specs=(
            P(("groups", "walk"), "elec", None),
            P("groups", None),
            P("groups", None),
            P("groups", None),
            P("groups", None),
        ),
        check_vma=False,
    )
```

```python
import functools
import math

import jax
import jax.numpy as jnp
from jax import lax
from jax.experimental import pallas as pl
from jax.experimental.pallas import tpu as pltpu
from jax.sharding import PartitionSpec as P


F32, BF16 = jnp.float32, jnp.bfloat16
LANES = 128
PACK = 8


def dot(a, b, dims=((1,), (0,))):
    return lax.dot_general(a, b, (dims, ((), ())), preferred_element_type=F32)


def dot_exact(a, b, dims=((1,), (0,))):
    return lax.dot_general(
        a, b, (dims, ((), ())), precision=lax.Precision.HIGHEST, preferred_element_type=F32
    )


def split(x):
    high = x.astype(BF16)
    return high, (x - high.astype(F32)).astype(BF16)


def iota(shape, axis):
    return lax.broadcasted_iota(jnp.int32, shape, axis)


def flag(condition):
    return jnp.where(condition, 1.0, 0.0).astype(F32)


def embed_kernel(total, hid, cot, pos, spin, w_in, w_out, w_pair, spin_bias, rates, out, big_out, *copies):
    walkers, rows, hidden_width = hid.shape
    proj, sense = [], []
    block = 2 * rows + 8
    n_rows = walkers * rows
    for w in range(walkers):
        proj.append(dot(hid[w], w_in[...], ((1,), (1,))))
        sense.append(dot(cot[w], w_out[...], ((1,), (1,))) / total)
        for k in range(hidden_width // LANES):
            at = block + k * n_rows + w * rows
            big_out[at : at + rows] = hid[w][:, k * LANES : (k + 1) * LANES].astype(F32)
            at = at + hidden_width // LANES * n_rows
            big_out[at : at + rows] = cot[w][:, k * LANES : (k + 1) * LANES].astype(F32)
    feats = []
    for c in range(3):
        x = pos[c]
        feats.append(jnp.cos(jnp.concatenate([x, x - 0.25], axis=0) * (2.0 * jnp.pi)))
    labels = jnp.broadcast_to(spin[...].astype(F32), (8, rows))
    feats.append(jnp.where(iota((8, rows), 0) == 0, labels, 1.0))
    feat = jnp.concatenate(feats, axis=0).T
    parts = [feat[8 * k : 8 * k + 8] for k in range(rows // 8)]
    parts.append(jnp.zeros((8, LANES - feat.shape[1] * (rows // 8)), F32))
    mine = jnp.concatenate(
        [
            jnp.concatenate(proj, axis=1),
            jnp.concatenate(sense, axis=1),
            jnp.concatenate(parts, axis=1),
        ],
        axis=0,
    )
    out[...] = mine
    big_out[0:block] = mine
    for ref, copy in zip((w_in, w_pair, spin_bias, rates), copies):
        copy[...] = ref[...]


def ripple(x, width):
    step = width
    while step < LANES:
        x = x + pltpu.roll(x, step, 1)
        step *= 2
    return x


def spread(x, w, width):
    return ripple(jnp.where(iota(x.shape, 1) // width == w, x, 0.0), width)


def wide(x):
    return jnp.concatenate([x, x], axis=1)


def thirds(x):
    high = x.astype(BF16)
    rest = x - high.astype(F32)
    middle = rest.astype(BF16)
    return high, middle, (rest - middle.astype(F32)).astype(BF16)


def features(packed, rows, feats):
    parts = [packed] + [pltpu.roll(packed, LANES - feats * k, 1) for k in range(1, rows // 8)]
    return jnp.concatenate(parts, axis=0)


def prepare_kernel(walkers, rows, own, w_pair, spin_bias, rates, basis_out, rows_out, *mix_out):
    width = w_pair.shape[0]
    lanes = PACK * width
    spin_at = 6 * walkers
    feats = spin_at + 8
    if mix_out:
        sel = flag(iota((LANES, width), 0) % width == iota((LANES, width), 1)).astype(BF16)
        sel_t = flag(iota((width, LANES), 1) % width == iota((width, LANES), 0)).astype(BF16)
        same = iota((LANES, LANES), 0) // width == iota((LANES, LANES), 1) // width
        high, low = [
            jnp.where(same, dot(dot(sel, part).astype(BF16), sel_t), 0.0) for part in split(w_pair[...])
        ]
        top = jnp.concatenate([high, low], axis=1)
        bottom = jnp.concatenate([high, jnp.zeros_like(high)], axis=1)
        mix_out[0][...] = jnp.concatenate([top, bottom], axis=0).astype(BF16)
    sel_wide = flag(iota((width, lanes), 1) % width == iota((width, lanes), 0))
    rate_row = dot_exact(rates[...], sel_wide) * (0.5 / (math.pi**2 * math.log(2.0)))
    bias_rows = dot_exact(spin_bias[...], sel_wide)
    bias_low, bias_step = bias_rows[0:1], bias_rows[1:2] - bias_rows[0:1]
    proj, sense = own[0:rows], own[rows : 2 * rows]
    feat = features(own[2 * rows : 2 * rows + 8], rows, feats)[:, :feats]
    feat_row = iota((feats, lanes), 0)
    tile = 0
    columns = [(wide(spread(proj, w, width)), wide(spread(sense, w, width))) for w in range(walkers)]
    groups, parts, spins = [], [], []
    for h in range(rows // PACK):
        group = flag(iota((rows, lanes), 1) // width + PACK * h == iota((rows, lanes), 0))
        cols = dot_exact(feat, group, ((0,), (0,)))
        spins.append(cols[spin_at : spin_at + 1])
        groups.append(group)
        parts.append(thirds(jnp.where(feat_row == spin_at + 1, -3.0, cols) * rate_row))
    for w in range(walkers):
        keep = ((feat_row < spin_at) & (feat_row % walkers == w)) | (feat_row == spin_at + 1)
        for h in range(rows // PACK):
            high, middle, low = [jnp.where(keep, p.astype(F32), 0.0).astype(BF16) for p in parts[h]]
            basis_out[:, tile * lanes : (tile + 1) * lanes] = jnp.concatenate(
                [high, middle, low, high, middle, high], axis=0
            )
            row_proj = jnp.sum(columns[w][0] * groups[h], axis=0, keepdims=True)
            row_sense = jnp.sum(columns[w][1] * groups[h], axis=0, keepdims=True)
            rows_out[8 * tile : 8 * tile + 8] = jnp.concatenate(
                [
                    row_sense,
                    row_proj + bias_low + (1.0 - spins[h]) * bias_step,
                    row_proj + bias_low + spins[h] * bias_step,
                    spins[h],
                    jnp.zeros((4, lanes), F32),
                ],
                axis=0,
            )
            tile += 1


def fold(x):
    return jnp.sum(x.reshape(x.shape[0] // 8, 8, x.shape[1]), axis=0)


def pair_kernel(walkers, width, rows, total, sets, *refs):
    side, gathered = refs[0], refs[1]
    bigs = refs[2 : 2 + sets]
    bases = refs[2 + sets : 2 + 2 * sets]
    row_sets = refs[2 + 2 * sets : 2 + 3 * sets]
    mix = refs[2 + 3 * sets]
    sens_out, keep_out, send_out, lhs, rhs = refs[3 + 3 * sets :]
    spin_at = 6 * walkers
    feats = spin_at + 8
    lanes = PACK * width
    per_walker = rows // PACK
    tiles = walkers * per_walker
    block = 2 * rows + 8
    starts = [block * s for s in range(gathered.shape[0] // block)]
    proj = jnp.concatenate([gathered[s : s + rows] for s in starts], axis=0)
    sense = jnp.concatenate([gathered[s + rows : s + 2 * rows] for s in starts], axis=0)
    feat = jnp.concatenate(
        [features(gathered[s + 2 * rows : s + block], rows, feats) for s in starts], axis=0
    )
    count = feat.shape[0]
    is_up = jnp.broadcast_to(feat[:, spin_at : spin_at + 1], (count, LANES)) > 0.5
    feat = jnp.where(iota(feat.shape, 1) < feats, feat, 0.0)
    high, middle, low = [p.astype(F32) for p in thirds(feat)]
    first = high + pltpu.roll(high, feats, 1) + pltpu.roll(high, 2 * feats, 1)
    first = first + pltpu.roll(middle, 3 * feats, 1)
    second = middle + pltpu.roll(low, feats, 1)
    left = jnp.concatenate([first, second[:, : 2 * feats]], axis=1).astype(BF16)
    halves = [slice(0, LANES), slice(LANES, lanes)]
    group = 2 * count * per_walker
    sums = [[None] * tiles for _ in range(sets)]
    for w in range(walkers):
        col_proj, col_sense = spread(proj, w, width), spread(sense, w, width)
        for n in range(sets):
            base = (w * sets + n) * group
            for k in range(per_walker):
                tile = w * per_walker + k
                radial = jnp.exp2(dot(left, bases[n][:, tile * lanes : (tile + 1) * lanes]))
                for i, half in enumerate(halves):
                    at = base + (2 * k + i) * count
                    high, low = split(radial[:, half])
                    lhs[at : at + count] = jnp.concatenate([high, low], axis=1)
            mixed = dot(lhs[base : base + group], mix[...])
            mixed = mixed[:, :LANES] + mixed[:, LANES:]
            for k in range(per_walker):
                tile = w * per_walker + k
                acc = []
                for i, half in enumerate(halves):
                    at = (2 * k + i) * count
                    row_sense = row_sets[n][8 * tile : 8 * tile + 1, half]
                    row_base = row_sets[n][8 * tile + 1 : 8 * tile + 2, half]
                    row_turn = row_sets[n][8 * tile + 2 : 8 * tile + 3, half]
                    z = mixed[at : at + count] + col_proj + jnp.where(is_up, row_turn, row_base)
                    if n == 0:
                        owner = iota((rows, LANES), 1) // width + PACK * k + i * (LANES // width)
                        far = jnp.where(owner == iota((rows, LANES), 0), 16384.0, 0.0)
                        z = jnp.concatenate([z[:rows] + far, z[rows:]], axis=0)
                    m = jnp.tanh(z)
                    slope = 1.0 - m * m
                    high, low = split(slope * row_sense)
                    rhs[base + at : base + at + count] = jnp.concatenate([high, low], axis=1)
                    acc.append((fold(slope), fold(jnp.where(is_up, slope, 0.0)), fold(slope * col_sense), fold(m)))
                sums[n][tile] = [jnp.concatenate([a, b], axis=1) for a, b in zip(*acc)]
    tn = ((0,), (0,))
    grams = dot(lhs[...], rhs[...], tn)
    lane8 = iota((8, lanes), 1) // width == iota((8, lanes), 0)
    lane = iota((8, LANES), 1) // width
    sens, mean = [], []
    same_row = jnp.zeros((1, lanes), F32)
    all_row = jnp.zeros((1, lanes), F32)

    def column(row):
        row = jnp.where(lane8, jnp.broadcast_to(row, (8, lanes)), 0.0)
        return ripple(row[:, :LANES] + row[:, LANES:], width)

    for n in range(sets):
        for t in range(tiles):
            slope, turn, col, act = [jnp.sum(x, axis=0, keepdims=True) for x in sums[n][t]]
            row_sense = row_sets[n][8 * t : 8 * t + 1]
            row_spin = row_sets[n][8 * t + 3 : 8 * t + 4]
            own = row_sense * slope
            sens.append(column(own + col))
            mean.append(column(act - 1.0 if n == 0 else act))
            all_row = all_row + own
            same_row = same_row + (1.0 - row_spin) * own
            same_row = same_row + (2.0 * row_spin - 1.0) * (row_sense * turn)
    sens = jnp.concatenate(sens, axis=0)
    mean = jnp.concatenate(mean, axis=0)
    n_rows = walkers * rows
    sens_out[...] = sens[:n_rows]
    lane_all = iota(sens.shape, 1) // width
    both = jnp.where(lane_all == 0, sens, jnp.where(lane_all == 1, mean, 0.0))
    high, low = split(both)
    chunks = (bigs[0].shape[0] - block) // n_rows
    inputs = [
        jnp.concatenate(
            [b[block + k * n_rows : block + (k + 1) * n_rows] for k in range(chunks)], axis=1
        )
        for b in bigs
    ]
    inputs = jnp.concatenate(inputs, axis=0).astype(BF16)
    weights = dot(high, inputs, tn) + dot(low, inputs, tn)
    hidden_width = inputs.shape[1] // 2
    in_part = weights[:width, :hidden_width]
    out_part = weights[width : 2 * width, hidden_width:] / total
    quad = grams[:LANES, :LANES] + grams[LANES:, :LANES] + (grams[:LANES, LANES:] + grams[LANES:, LANES:])
    pair = quad[0:width]
    for k in range(1, LANES // width):
        pair = pair + pltpu.roll(quad[k * width : (k + 1) * width], LANES - k * width, 1)
    tail = jnp.where(lane == 0, pair[0:8], 0.0)
    for k in range(1, width // 8):
        tail = tail + jnp.where(lane == k, pltpu.roll(pair[8 * k : 8 * k + 8], k * width, 1), 0.0)
    pick = iota((8, lanes), 0)
    bias = jnp.where(
        pick == 0,
        jnp.broadcast_to(all_row - same_row, (8, lanes)),
        jnp.where(pick == 1, jnp.broadcast_to(same_row, (8, lanes)), 0.0),
    )
    bias = ripple(bias[:, :LANES] + bias[:, LANES:], width)
    half = hidden_width // 2
    low_half = jnp.concatenate([in_part[:, :half], out_part[:, :half], tail], axis=0)
    high_half = jnp.concatenate([in_part[:, half:], out_part[:, half:], bias], axis=0)
    first = side[0] == 0
    flat = low_half.shape[0]
    keep_out[0:flat] = jnp.where(first, low_half, high_half)
    send_out[...] = jnp.where(first, high_half, low_half)
    place = iota((rows, LANES), 1) // width
    for n in range(1, sets):
        packed = jnp.zeros((rows, LANES), F32)
        for w in range(walkers):
            part = sens[n * n_rows + w * rows : n * n_rows + (w + 1) * rows]
            packed = packed + jnp.where(place == w, part, 0.0)
        at = flat + (n - 1) * rows
        keep_out[at : at + rows] = packed


def hidden_kernel(offsets, sens, w_in, *refs):
    received, grad_out = refs[:-1], refs[-1]
    walkers, rows, _ = grad_out.shape
    width = w_in.shape[0]
    total = []
    for w in range(walkers):
        part = sens[w * rows : (w + 1) * rows]
        for at, ref in zip(offsets, received):
            part = part + spread(ref[at : at + rows], w, width)
        total.append(part)
    high, low = split(jnp.concatenate(total, axis=0))
    both = jnp.concatenate([high[:, :width], low[:, :width]], axis=1)
    grad = dot(both, jnp.concatenate([w_in[...], w_in[...]], axis=0))
    for w in range(walkers):
        grad_out[w] = grad[w * rows : (w + 1) * rows].astype(BF16)


def finish_kernel(side, mine, other, w_in_grad, w_pair_grad, bias_grad, w_out_grad):
    width = w_pair_grad.shape[0]
    first = side[0] == 0
    low = jnp.where(first, mine[...], other[...])
    high = jnp.where(first, other[...], mine[...])
    full = jnp.concatenate([low, high], axis=1)
    w_in_grad[...] = full[:width]
    w_out_grad[...] = full[width : 2 * width]
    tail = full[2 * width :]
    for k in range(width // 8):
        w_pair_grad[8 * k : 8 * k + 8] = tail[:, k * width : (k + 1) * width]
    at = (width // 8) * width
    bias_grad[...] = tail[0:2, at : at + width]


VMEM = pl.BlockSpec(memory_space=pltpu.VMEM)
SMEM = pl.BlockSpec(memory_space=pltpu.SMEM)


def near(x):
    return pltpu.with_memory_space_constraint(x, pltpu.VMEM)


def swap(x, axis, size, mask):
    return lax.ppermute(x, axis, [(i, i ^ mask) for i in range(size)])


def stages(blocks):
    groups, top = [], blocks
    while top > 2:
        groups.append((top // 4, top // 2, 3 * top // 4))
        top //= 4
    if top == 2:
        groups.append((1,))
    return groups


def join(mine, got):
    mine = mine + got[0]
    return mine + (got[1] + got[2]) if len(got) == 3 else mine


def on_device(hidden, cotangent, positions, spins, w_in, w_pair, spin_bias, rates, w_out):
    blocks = lax.axis_size("elec")
    walkers, rows, hidden_width = hidden.shape
    width = w_in.shape[1]
    total = rows * blocks
    side = lax.axis_index("walk").astype(jnp.int32).reshape(1)
    block = 2 * rows + 8
    n_rows = walkers * rows
    lanes = PACK * width
    tiles = n_rows // PACK
    groups = stages(blocks)
    col_groups, row_masks = groups[:-1], groups[-1]
    sets = 1 + len(row_masks)
    payload, big, *params = pl.pallas_call(
        functools.partial(embed_kernel, total),
        out_shape=(
            pltpu.VMEM((block, LANES), F32),
            pltpu.VMEM((block + n_rows * 2 * hidden_width // LANES, LANES), F32),
            pltpu.VMEM((width, hidden_width), BF16),
            pltpu.VMEM((width, width), F32),
            pltpu.VMEM((2, width), F32),
            pltpu.VMEM((1, width), F32),
        ),
        in_specs=[VMEM] * 9,
        out_specs=(VMEM,) * 6,
        name="embed",
    )(
        hidden,
        cotangent,
        positions.transpose(1, 0, 2),
        spins.reshape(1, rows),
        w_in.T,
        w_out,
        w_pair,
        spin_bias,
        rates.reshape(1, width),
    )
    w_in_near, *params = [near(p) for p in params]
    bigs = [big] + [swap(big, "elec", blocks, m) for m in row_masks]
    gathered = [payload]
    for masks in col_groups:
        whole = gathered[0] if len(gathered) == 1 else jnp.concatenate(gathered, axis=0)
        gathered = [whole] + [swap(whole, "elec", blocks, m) for m in masks]
    columns = gathered[0] if len(gathered) == 1 else jnp.concatenate(gathered, axis=0)
    depth = 6 * (6 * walkers + 8)

    def prepare(source, first):
        extra = (pltpu.VMEM((lanes, lanes), BF16),) if first else ()
        return pl.pallas_call(
            functools.partial(prepare_kernel, walkers, rows),
            out_shape=(
                pltpu.VMEM((depth, tiles * lanes), BF16),
                pltpu.VMEM((8 * tiles, lanes), F32),
            )
            + extra,
            in_specs=[VMEM] * 4,
            out_specs=(VMEM,) * (2 + len(extra)),
            name="prepare_own" if first else "prepare_row",
        )(near(source), *params)

    basis, row_terms, mix = prepare(payload, True)
    bases, row_sets = [basis], [row_terms]
    for source in bigs[1:]:
        basis, row_terms = prepare(source, False)
        bases.append(basis)
        row_sets.append(row_terms)
    flat = 2 * width + 8
    tall = flat + (sets - 1) * rows
    depth = columns.shape[0] // block * rows * 2 * tiles * sets
    operands = [columns, *bigs, *bases, *row_sets, mix]
    sens, keep, send = pl.pallas_call(
        functools.partial(pair_kernel, walkers, width, rows, total, sets),
        out_shape=(
            pltpu.VMEM((n_rows, LANES), F32),
            pltpu.VMEM((tall, LANES), F32),
            pltpu.VMEM((flat, LANES), F32),
        ),
        in_specs=[SMEM] + [VMEM] * len(operands),
        out_specs=(VMEM,) * 3,
        scratch_shapes=[pltpu.VMEM((depth, 2 * LANES), BF16)] * 2,
        name="pairs",
    )(side, *[near(x) for x in operands])
    near_part = swap(send, "walk", 2, 1)
    got = [swap(keep, "elec", blocks, m) for m in row_masks]
    cross = [swap(send, ("elec", "walk"), 2 * blocks, 2 * m + 1) for m in row_masks]
    offsets = tuple(flat + n * rows for n in range(len(got)))
    grad = pl.pallas_call(
        functools.partial(hidden_kernel, offsets),
        out_shape=jax.ShapeDtypeStruct(hidden.shape, BF16),
        in_specs=[VMEM] * (2 + len(got)),
        out_specs=VMEM,
        name="hidden_grad",
    )(near(sens), w_in_near, *[near(g) for g in got])
    mine = join(keep[:flat] + near_part, [g[:flat] + c for g, c in zip(got, cross)])
    for masks in reversed(col_groups):
        got = [swap(mine, "elec", blocks, m) for m in masks]
        mine = join(mine, got)
    other = swap(mine, "walk", 2, 1)
    w_in_grad, w_pair_grad, spin_bias_grad, w_out_grad = pl.pallas_call(
        finish_kernel,
        out_shape=(
            jax.ShapeDtypeStruct((width, hidden_width), F32),
            jax.ShapeDtypeStruct((width, width), F32),
            jax.ShapeDtypeStruct((2, width), F32),
            jax.ShapeDtypeStruct((width, hidden_width), F32),
        ),
        in_specs=[SMEM, VMEM, VMEM],
        out_specs=(VMEM,) * 4,
        name="finish",
    )(side, near(mine), near(other))
    return (grad, w_in_grad.T, w_pair_grad, spin_bias_grad, w_out_grad)


def solution(mesh):
    return jax.shard_map(
        on_device,
        mesh=mesh,
        in_specs=(
            P(("groups", "walk"), "elec", None),
            P(("groups", "walk"), "elec", None),
            P(("groups", "walk"), None, "elec"),
            P(("groups", "elec")),
            P(),
            P(),
            P(),
            P(),
            P(),
        ),
        out_specs=(
            P(("groups", "walk"), "elec", None),
            P("groups", None),
            P("groups", None),
            P("groups", None),
            P("groups", None),
        ),
        check_vma=False,
    )
```

```python
import functools
import math

import jax
import jax.numpy as jnp
from jax import lax
from jax.experimental import pallas as pl
from jax.experimental.pallas import tpu as pltpu
from jax.sharding import PartitionSpec as P


F32, BF16 = jnp.float32, jnp.bfloat16
LANES = 128
PACK = 8


def dot(a, b, dims=((1,), (0,))):
    return lax.dot_general(a, b, (dims, ((), ())), preferred_element_type=F32)


def dot_exact(a, b, dims=((1,), (0,))):
    return lax.dot_general(
        a, b, (dims, ((), ())), precision=lax.Precision.HIGHEST, preferred_element_type=F32
    )


def split(x):
    high = x.astype(BF16)
    return high, (x - high.astype(F32)).astype(BF16)


def iota(shape, axis):
    return lax.broadcasted_iota(jnp.int32, shape, axis)


def flag(condition):
    return jnp.where(condition, 1.0, 0.0).astype(F32)


def embed_kernel(total, hid, cot, pos, spin, w_in, w_out, w_pair, spin_bias, rates, out, big_out, *copies):
    walkers, rows, hidden_width = hid.shape
    proj, sense = [], []
    block = 2 * rows + 8
    n_rows = walkers * rows
    for w in range(walkers):
        proj.append(dot(hid[w], w_in[...], ((1,), (1,))))
        sense.append(dot(cot[w], w_out[...], ((1,), (1,))) / total)
        for k in range(hidden_width // LANES):
            at = block + k * n_rows + w * rows
            big_out[at : at + rows] = hid[w][:, k * LANES : (k + 1) * LANES].astype(F32)
            at = at + hidden_width // LANES * n_rows
            big_out[at : at + rows] = cot[w][:, k * LANES : (k + 1) * LANES].astype(F32)
    feats = []
    for c in range(3):
        x = pos[c]
        feats.append(jnp.cos(jnp.concatenate([x, x - 0.25], axis=0) * (2.0 * jnp.pi)))
    labels = jnp.broadcast_to(spin[...].astype(F32), (8, rows))
    feats.append(jnp.where(iota((8, rows), 0) == 0, labels, 1.0))
    feat = jnp.concatenate(feats, axis=0).T
    parts = [feat[8 * k : 8 * k + 8] for k in range(rows // 8)]
    parts.append(jnp.zeros((8, LANES - feat.shape[1] * (rows // 8)), F32))
    mine = jnp.concatenate(
        [
            jnp.concatenate(proj, axis=1),
            jnp.concatenate(sense, axis=1),
            jnp.concatenate(parts, axis=1),
        ],
        axis=0,
    )
    out[...] = mine
    big_out[0:block] = mine
    for ref, copy in zip((w_in, w_pair, spin_bias, rates), copies):
        copy[...] = ref[...]


def ripple(x, width):
    step = width
    while step < LANES:
        x = x + pltpu.roll(x, step, 1)
        step *= 2
    return x


def spread(x, w, width):
    return ripple(jnp.where(iota(x.shape, 1) // width == w, x, 0.0), width)


def wide(x):
    return jnp.concatenate([x, x], axis=1)


def thirds(x):
    high = x.astype(BF16)
    rest = x - high.astype(F32)
    middle = rest.astype(BF16)
    return high, middle, (rest - middle.astype(F32)).astype(BF16)


def features(packed, rows, feats):
    parts = [packed] + [pltpu.roll(packed, LANES - feats * k, 1) for k in range(1, rows // 8)]
    return jnp.concatenate(parts, axis=0)


def prepare_kernel(walkers, rows, own, w_pair, spin_bias, rates, basis_out, rows_out, *mix_out):
    width = w_pair.shape[0]
    lanes = PACK * width
    spin_at = 6 * walkers
    feats = spin_at + 8
    if mix_out:
        sel = flag(iota((LANES, width), 0) % width == iota((LANES, width), 1)).astype(BF16)
        sel_t = flag(iota((width, LANES), 1) % width == iota((width, LANES), 0)).astype(BF16)
        same = iota((LANES, LANES), 0) // width == iota((LANES, LANES), 1) // width
        high, low = [
            jnp.where(same, dot(dot(sel, part).astype(BF16), sel_t), 0.0) for part in split(w_pair[...])
        ]
        top = jnp.concatenate([high, low], axis=1)
        bottom = jnp.concatenate([high, jnp.zeros_like(high)], axis=1)
        mix_out[0][...] = jnp.concatenate([top, bottom], axis=0).astype(BF16)
    sel_wide = flag(iota((width, lanes), 1) % width == iota((width, lanes), 0))
    rate_row = dot_exact(rates[...], sel_wide) * (0.5 / (math.pi**2 * math.log(2.0)))
    bias_rows = dot_exact(spin_bias[...], sel_wide)
    bias_low, bias_step = bias_rows[0:1], bias_rows[1:2] - bias_rows[0:1]
    proj, sense = own[0:rows], own[rows : 2 * rows]
    feat = features(own[2 * rows : 2 * rows + 8], rows, feats)[:, :feats]
    feat_row = iota((feats, lanes), 0)
    tile = 0
    columns = [(wide(spread(proj, w, width)), wide(spread(sense, w, width))) for w in range(walkers)]
    groups, parts, spins = [], [], []
    for h in range(rows // PACK):
        group = flag(iota((rows, lanes), 1) // width + PACK * h == iota((rows, lanes), 0))
        cols = dot_exact(feat, group, ((0,), (0,)))
        spins.append(cols[spin_at : spin_at + 1])
        groups.append(group)
        parts.append(thirds(jnp.where(feat_row == spin_at + 1, -3.0, cols) * rate_row))
    for w in range(walkers):
        keep = ((feat_row < spin_at) & (feat_row % walkers == w)) | (feat_row == spin_at + 1)
        for h in range(rows // PACK):
            high, middle, low = [jnp.where(keep, p.astype(F32), 0.0).astype(BF16) for p in parts[h]]
            basis_out[:, tile * lanes : (tile + 1) * lanes] = jnp.concatenate(
                [high, middle, low, high, middle, high], axis=0
            )
            row_proj = jnp.sum(columns[w][0] * groups[h], axis=0, keepdims=True)
            row_sense = jnp.sum(columns[w][1] * groups[h], axis=0, keepdims=True)
            rows_out[8 * tile : 8 * tile + 8] = jnp.concatenate(
                [
                    row_sense,
                    row_proj + bias_low + (1.0 - spins[h]) * bias_step,
                    row_proj + bias_low + spins[h] * bias_step,
                    spins[h],
                    jnp.zeros((4, lanes), F32),
                ],
                axis=0,
            )
            tile += 1


def fold(x):
    return jnp.sum(x.reshape(x.shape[0] // 8, 8, x.shape[1]), axis=0)


def pair_kernel(walkers, width, rows, total, sets, *refs):
    side, gathered = refs[0], refs[1]
    bigs = refs[2 : 2 + sets]
    bases = refs[2 + sets : 2 + 2 * sets]
    row_sets = refs[2 + 2 * sets : 2 + 3 * sets]
    mix = refs[2 + 3 * sets]
    sens_out, keep_out, send_out, lhs, rhs = refs[3 + 3 * sets :]
    spin_at = 6 * walkers
    feats = spin_at + 8
    lanes = PACK * width
    per_walker = rows // PACK
    tiles = walkers * per_walker
    block = 2 * rows + 8
    starts = [block * s for s in range(gathered.shape[0] // block)]
    proj = jnp.concatenate([gathered[s : s + rows] for s in starts], axis=0)
    sense = jnp.concatenate([gathered[s + rows : s + 2 * rows] for s in starts], axis=0)
    feat = jnp.concatenate(
        [features(gathered[s + 2 * rows : s + block], rows, feats) for s in starts], axis=0
    )
    count = feat.shape[0]
    is_up = jnp.broadcast_to(feat[:, spin_at : spin_at + 1], (count, LANES)) > 0.5
    feat = jnp.where(iota(feat.shape, 1) < feats, feat, 0.0)
    high, middle, low = [p.astype(F32) for p in thirds(feat)]
    first = high + pltpu.roll(high, feats, 1) + pltpu.roll(high, 2 * feats, 1)
    first = first + pltpu.roll(middle, 3 * feats, 1)
    second = middle + pltpu.roll(low, feats, 1)
    left = jnp.concatenate([first, second[:, : 2 * feats]], axis=1).astype(BF16)
    halves = [slice(0, LANES), slice(LANES, lanes)]
    group = 2 * count * per_walker
    sums = [[None] * tiles for _ in range(sets)]
    for w in range(walkers):
        col_proj, col_sense = spread(proj, w, width), spread(sense, w, width)
        for n in range(sets):
            base = (w * sets + n) * group
            for k in range(per_walker):
                tile = w * per_walker + k
                radial = jnp.exp2(dot(left, bases[n][:, tile * lanes : (tile + 1) * lanes]))
                for i, half in enumerate(halves):
                    at = base + (2 * k + i) * count
                    high, low = split(radial[:, half])
                    lhs[at : at + count] = jnp.concatenate([high, low], axis=1)
            mixed = dot(lhs[base : base + group], mix[...])
            mixed = mixed[:, :LANES] + mixed[:, LANES:]
            for k in range(per_walker):
                tile = w * per_walker + k
                acc = []
                for i, half in enumerate(halves):
                    at = (2 * k + i) * count
                    row_sense = row_sets[n][8 * tile : 8 * tile + 1, half]
                    row_base = row_sets[n][8 * tile + 1 : 8 * tile + 2, half]
                    row_turn = row_sets[n][8 * tile + 2 : 8 * tile + 3, half]
                    z = mixed[at : at + count] + col_proj + jnp.where(is_up, row_turn, row_base)
                    if n == 0:
                        owner = iota((rows, LANES), 1) // width + PACK * k + i * (LANES // width)
                        far = jnp.where(owner == iota((rows, LANES), 0), 16384.0, 0.0)
                        z = jnp.concatenate([z[:rows] + far, z[rows:]], axis=0)
                    m = jnp.tanh(z)
                    slope = 1.0 - m * m
                    high, low = split(slope * row_sense)
                    rhs[base + at : base + at + count] = jnp.concatenate([high, low], axis=1)
                    acc.append((fold(slope), fold(jnp.where(is_up, slope, 0.0)), fold(slope * col_sense), fold(m)))
                sums[n][tile] = [jnp.concatenate([a, b], axis=1) for a, b in zip(*acc)]
    tn = ((0,), (0,))
    grams = dot(lhs[...], rhs[...], tn)
    lane8 = iota((8, lanes), 1) // width == iota((8, lanes), 0)
    lane = iota((8, LANES), 1) // width
    sens, mean = [], []
    same_row = jnp.zeros((1, lanes), F32)
    all_row = jnp.zeros((1, lanes), F32)

    def column(row):
        row = jnp.where(lane8, jnp.broadcast_to(row, (8, lanes)), 0.0)
        return ripple(row[:, :LANES] + row[:, LANES:], width)

    for n in range(sets):
        for t in range(tiles):
            slope, turn, col, act = [jnp.sum(x, axis=0, keepdims=True) for x in sums[n][t]]
            row_sense = row_sets[n][8 * t : 8 * t + 1]
            row_spin = row_sets[n][8 * t + 3 : 8 * t + 4]
            own = row_sense * slope
            sens.append(column(own + col))
            mean.append(column(act - 1.0 if n == 0 else act))
            all_row = all_row + own
            same_row = same_row + (1.0 - row_spin) * own
            same_row = same_row + (2.0 * row_spin - 1.0) * (row_sense * turn)
    sens = jnp.concatenate(sens, axis=0)
    mean = jnp.concatenate(mean, axis=0)
    n_rows = walkers * rows
    sens_out[...] = sens[:n_rows]
    lane_all = iota(sens.shape, 1) // width
    both = jnp.where(lane_all == 0, sens, jnp.where(lane_all == 1, mean, 0.0))
    high, low = split(both)
    chunks = (bigs[0].shape[0] - block) // n_rows
    inputs = [
        jnp.concatenate(
            [b[block + k * n_rows : block + (k + 1) * n_rows] for k in range(chunks)], axis=1
        )
        for b in bigs
    ]
    inputs = jnp.concatenate(inputs, axis=0).astype(BF16)
    weights = dot(high, inputs, tn) + dot(low, inputs, tn)
    hidden_width = inputs.shape[1] // 2
    in_part = weights[:width, :hidden_width]
    out_part = weights[width : 2 * width, hidden_width:] / total
    quad = grams[:LANES, :LANES] + grams[LANES:, :LANES] + (grams[:LANES, LANES:] + grams[LANES:, LANES:])
    pair = quad[0:width]
    for k in range(1, LANES // width):
        pair = pair + pltpu.roll(quad[k * width : (k + 1) * width], LANES - k * width, 1)
    tail = jnp.where(lane == 0, pair[0:8], 0.0)
    for k in range(1, width // 8):
        tail = tail + jnp.where(lane == k, pltpu.roll(pair[8 * k : 8 * k + 8], k * width, 1), 0.0)
    pick = iota((8, lanes), 0)
    bias = jnp.where(
        pick == 0,
        jnp.broadcast_to(all_row - same_row, (8, lanes)),
        jnp.where(pick == 1, jnp.broadcast_to(same_row, (8, lanes)), 0.0),
    )
    bias = ripple(bias[:, :LANES] + bias[:, LANES:], width)
    half = hidden_width // 2
    low_half = jnp.concatenate([in_part[:, :half], out_part[:, :half], tail], axis=0)
    high_half = jnp.concatenate([in_part[:, half:], out_part[:, half:], bias], axis=0)
    first = side[0] == 0
    flat = low_half.shape[0]
    keep_out[0:flat] = jnp.where(first, low_half, high_half)
    send_out[...] = jnp.where(first, high_half, low_half)
    place = iota((rows, LANES), 1) // width
    for n in range(1, sets):
        packed = jnp.zeros((rows, LANES), F32)
        for w in range(walkers):
            part = sens[n * n_rows + w * rows : n * n_rows + (w + 1) * rows]
            packed = packed + jnp.where(place == w, part, 0.0)
        at = flat + (n - 1) * rows
        keep_out[at : at + rows] = packed


def hidden_kernel(offsets, sens, w_in, *refs):
    received, grad_out = refs[:-1], refs[-1]
    walkers, rows, _ = grad_out.shape
    width = w_in.shape[0]
    total = []
    for w in range(walkers):
        part = sens[w * rows : (w + 1) * rows]
        for at, ref in zip(offsets, received):
            part = part + spread(ref[at : at + rows], w, width)
        total.append(part)
    high, low = split(jnp.concatenate(total, axis=0))
    both = jnp.concatenate([high[:, :width], low[:, :width]], axis=1)
    grad = dot(both, jnp.concatenate([w_in[...], w_in[...]], axis=0))
    for w in range(walkers):
        grad_out[w] = grad[w * rows : (w + 1) * rows].astype(BF16)


def finish_kernel(side, mine, other, w_in_grad, w_pair_grad, bias_grad, w_out_grad):
    width = w_pair_grad.shape[0]
    first = side[0] == 0
    low = jnp.where(first, mine[...], other[...])
    high = jnp.where(first, other[...], mine[...])
    full = jnp.concatenate([low, high], axis=1)
    w_in_grad[...] = full[:width]
    w_out_grad[...] = full[width : 2 * width]
    tail = full[2 * width :]
    for k in range(width // 8):
        w_pair_grad[8 * k : 8 * k + 8] = tail[:, k * width : (k + 1) * width]
    at = (width // 8) * width
    bias_grad[...] = tail[0:2, at : at + width]


VMEM = pl.BlockSpec(memory_space=pltpu.VMEM)
SMEM = pl.BlockSpec(memory_space=pltpu.SMEM)


def near(x):
    return pltpu.with_memory_space_constraint(x, pltpu.VMEM)


def swap(x, axis, size, mask):
    return lax.ppermute(x, axis, [(i, i ^ mask) for i in range(size)])


def stages(blocks):
    row = min(2, blocks // 2)
    bits = [1 << k for k in range(blocks.bit_length() - 1) if 1 << k != row]
    groups = []
    while len(bits) > 1:
        high, low = bits.pop(), bits.pop()
        groups.append((low, high, low ^ high))
    if bits:
        groups.append((bits.pop(),))
    return groups + [(row,)]


def join(mine, got):
    mine = mine + got[0]
    return mine + (got[1] + got[2]) if len(got) == 3 else mine


def on_device(hidden, cotangent, positions, spins, w_in, w_pair, spin_bias, rates, w_out):
    blocks = lax.axis_size("elec")
    walkers, rows, hidden_width = hidden.shape
    width = w_in.shape[1]
    total = rows * blocks
    block = 2 * rows + 8
    n_rows = walkers * rows
    lanes = PACK * width
    tiles = n_rows // PACK
    groups = stages(blocks)
    col_groups, row_masks = groups[:-1], groups[-1]
    turns = sum(masks[1] for masks in col_groups if len(masks) == 3)
    side = lax.axis_index("walk").astype(jnp.int32)
    for bit in range(blocks.bit_length()):
        if turns >> bit & 1:
            side = side ^ (lax.axis_index("elec").astype(jnp.int32) >> bit & 1)
    side = side.reshape(1)
    sets = 1 + len(row_masks)
    payload, big, *params = pl.pallas_call(
        functools.partial(embed_kernel, total),
        out_shape=(
            pltpu.VMEM((block, LANES), F32),
            pltpu.VMEM((block + n_rows * 2 * hidden_width // LANES, LANES), F32),
            pltpu.VMEM((width, hidden_width), BF16),
            pltpu.VMEM((width, width), F32),
            pltpu.VMEM((2, width), F32),
            pltpu.VMEM((1, width), F32),
        ),
        in_specs=[VMEM] * 9,
        out_specs=(VMEM,) * 6,
        name="embed",
    )(
        hidden,
        cotangent,
        positions.transpose(1, 0, 2),
        spins.reshape(1, rows),
        w_in.T,
        w_out,
        w_pair,
        spin_bias,
        rates.reshape(1, width),
    )
    w_in_near, *params = [near(p) for p in params]
    bigs = [big] + [swap(big, "elec", blocks, m) for m in row_masks]
    gathered = [payload]
    for masks in col_groups:
        whole = gathered[0] if len(gathered) == 1 else jnp.concatenate(gathered, axis=0)
        gathered = [whole] + [swap(whole, "elec", blocks, m) for m in masks]
    columns = gathered[0] if len(gathered) == 1 else jnp.concatenate(gathered, axis=0)
    depth = 6 * (6 * walkers + 8)

    def prepare(source, first):
        extra = (pltpu.VMEM((lanes, lanes), BF16),) if first else ()
        return pl.pallas_call(
            functools.partial(prepare_kernel, walkers, rows),
            out_shape=(
                pltpu.VMEM((depth, tiles * lanes), BF16),
                pltpu.VMEM((8 * tiles, lanes), F32),
            )
            + extra,
            in_specs=[VMEM] * 4,
            out_specs=(VMEM,) * (2 + len(extra)),
            name="prepare_own" if first else "prepare_row",
        )(near(source), *params)

    basis, row_terms, mix = prepare(payload, True)
    bases, row_sets = [basis], [row_terms]
    for source in bigs[1:]:
        basis, row_terms = prepare(source, False)
        bases.append(basis)
        row_sets.append(row_terms)
    flat = 2 * width + 8
    tall = flat + (sets - 1) * rows
    depth = columns.shape[0] // block * rows * 2 * tiles * sets
    operands = [columns, *bigs, *bases, *row_sets, mix]
    sens, keep, send = pl.pallas_call(
        functools.partial(pair_kernel, walkers, width, rows, total, sets),
        out_shape=(
            pltpu.VMEM((n_rows, LANES), F32),
            pltpu.VMEM((tall, LANES), F32),
            pltpu.VMEM((flat, LANES), F32),
        ),
        in_specs=[SMEM] + [VMEM] * len(operands),
        out_specs=(VMEM,) * 3,
        scratch_shapes=[pltpu.VMEM((depth, 2 * LANES), BF16)] * 2,
        name="pairs",
    )(side, *[near(x) for x in operands])
    near_part = swap(send, "walk", 2, 1)
    got = [swap(keep, "elec", blocks, m) for m in row_masks]
    cross = [swap(send, ("elec", "walk"), 2 * blocks, 2 * m + 1) for m in row_masks]
    offsets = tuple(flat + n * rows for n in range(len(got)))
    grad = pl.pallas_call(
        functools.partial(hidden_kernel, offsets),
        out_shape=jax.ShapeDtypeStruct(hidden.shape, BF16),
        in_specs=[VMEM] * (2 + len(got)),
        out_specs=VMEM,
        name="hidden_grad",
    )(near(sens), w_in_near, *[near(g) for g in got])
    mine = join(keep[:flat] + near_part, [g[:flat] + c for g, c in zip(got, cross)])
    for masks in reversed(col_groups):
        got = [
            swap(mine, ("elec", "walk"), 2 * blocks, 2 * m + (m & turns).bit_count() % 2)
            for m in masks
        ]
        mine = join(mine, got)
    other = swap(mine, "walk", 2, 1)
    w_in_grad, w_pair_grad, spin_bias_grad, w_out_grad = pl.pallas_call(
        finish_kernel,
        out_shape=(
            jax.ShapeDtypeStruct((width, hidden_width), F32),
            jax.ShapeDtypeStruct((width, width), F32),
            jax.ShapeDtypeStruct((2, width), F32),
            jax.ShapeDtypeStruct((width, hidden_width), F32),
        ),
        in_specs=[SMEM, VMEM, VMEM],
        out_specs=(VMEM,) * 4,
        name="finish",
    )(side, near(mine), near(other))
    return (grad, w_in_grad.T, w_pair_grad, spin_bias_grad, w_out_grad)


def solution(mesh):
    return jax.shard_map(
        on_device,
        mesh=mesh,
        in_specs=(
            P(("groups", "walk"), "elec", None),
            P(("groups", "walk"), "elec", None),
            P(("groups", "walk"), None, "elec"),
            P(("groups", "elec")),
            P(),
            P(),
            P(),
            P(),
            P(),
        ),
        out_specs=(
            P(("groups", "walk"), "elec", None),
            P("groups", None),
            P("groups", None),
            P("groups", None),
            P("groups", None),
        ),
        check_vma=False,
    )
```

```python
import functools
import math

import jax
import jax.numpy as jnp
from jax import lax
from jax.experimental import pallas as pl
from jax.experimental.pallas import tpu as pltpu
from jax.sharding import PartitionSpec as P


F32, BF16 = jnp.float32, jnp.bfloat16
LANES = 128
PACK = 8


def dot(a, b, dims=((1,), (0,))):
    return lax.dot_general(a, b, (dims, ((), ())), preferred_element_type=F32)


def dot_exact(a, b, dims=((1,), (0,))):
    return lax.dot_general(
        a, b, (dims, ((), ())), precision=lax.Precision.HIGHEST, preferred_element_type=F32
    )


def split(x):
    high = x.astype(BF16)
    return high, (x - high.astype(F32)).astype(BF16)


def iota(shape, axis):
    return lax.broadcasted_iota(jnp.int32, shape, axis)


def flag(condition):
    return jnp.where(condition, 1.0, 0.0).astype(F32)


def embed_kernel(total, hid, cot, pos, spin, w_in, w_out, w_pair, spin_bias, rates, out, big_out, *copies):
    walkers, rows, hidden_width = hid.shape
    proj, sense = [], []
    block = 2 * rows + 8
    n_rows = walkers * rows
    for w in range(walkers):
        proj.append(dot(hid[w], w_in[...], ((1,), (1,))))
        sense.append(dot(cot[w], w_out[...], ((1,), (1,))) / total)
        for k in range(hidden_width // LANES):
            at = block + k * n_rows + w * rows
            big_out[at : at + rows] = hid[w][:, k * LANES : (k + 1) * LANES].astype(F32)
            at = at + hidden_width // LANES * n_rows
            big_out[at : at + rows] = cot[w][:, k * LANES : (k + 1) * LANES].astype(F32)
    feats = []
    for c in range(3):
        x = pos[c]
        feats.append(jnp.cos(jnp.concatenate([x, x - 0.25], axis=0) * (2.0 * jnp.pi)))
    labels = jnp.broadcast_to(spin[...].astype(F32), (8, rows))
    feats.append(jnp.where(iota((8, rows), 0) == 0, labels, 1.0))
    feat = jnp.concatenate(feats, axis=0).T
    parts = [feat[8 * k : 8 * k + 8] for k in range(rows // 8)]
    parts.append(jnp.zeros((8, LANES - feat.shape[1] * (rows // 8)), F32))
    mine = jnp.concatenate(
        [
            jnp.concatenate(proj, axis=1),
            jnp.concatenate(sense, axis=1),
            jnp.concatenate(parts, axis=1),
        ],
        axis=0,
    )
    out[...] = mine
    big_out[0:block] = mine
    for ref, copy in zip((w_in, w_pair, spin_bias, rates), copies):
        copy[...] = ref[...]


def ripple(x, width):
    step = width
    while step < LANES:
        x = x + pltpu.roll(x, step, 1)
        step *= 2
    return x


def spread(x, w, width):
    return ripple(jnp.where(iota(x.shape, 1) // width == w, x, 0.0), width)


def wide(x):
    return jnp.concatenate([x, x], axis=1)


def thirds(x):
    high = x.astype(BF16)
    rest = x - high.astype(F32)
    middle = rest.astype(BF16)
    return high, middle, (rest - middle.astype(F32)).astype(BF16)


def features(packed, rows, feats):
    parts = [packed] + [pltpu.roll(packed, LANES - feats * k, 1) for k in range(1, rows // 8)]
    return jnp.concatenate(parts, axis=0)


def prepare_kernel(walkers, rows, own, w_pair, spin_bias, rates, basis_out, rows_out, *mix_out):
    width = w_pair.shape[0]
    lanes = PACK * width
    spin_at = 6 * walkers
    feats = spin_at + 8
    if mix_out:
        sel = flag(iota((LANES, width), 0) % width == iota((LANES, width), 1)).astype(BF16)
        sel_t = flag(iota((width, LANES), 1) % width == iota((width, LANES), 0)).astype(BF16)
        same = iota((LANES, LANES), 0) // width == iota((LANES, LANES), 1) // width
        high, low = [
            jnp.where(same, dot(dot(sel, part).astype(BF16), sel_t), 0.0) for part in split(w_pair[...])
        ]
        top = jnp.concatenate([high, low], axis=1)
        bottom = jnp.concatenate([high, jnp.zeros_like(high)], axis=1)
        mix_out[0][...] = jnp.concatenate([top, bottom], axis=0).astype(BF16)
    if mix_out:
        sel_wide = flag(iota((width, lanes), 1) % width == iota((width, lanes), 0))
        rate_row = dot_exact(rates[...], sel_wide) * (0.5 / (math.pi**2 * math.log(2.0)))
        bias_rows = dot_exact(spin_bias[...], sel_wide)
        mix_out[1][...] = jnp.concatenate([rate_row, bias_rows], axis=0)
    else:
        rate_row, bias_rows = rates[...], spin_bias[...]
    bias_low, bias_step = bias_rows[0:1], bias_rows[1:2] - bias_rows[0:1]
    proj, sense = own[0:rows], own[rows : 2 * rows]
    feat = features(own[2 * rows : 2 * rows + 8], rows, feats)[:, :feats]
    feat_row = iota((feats, lanes), 0)
    tile = 0
    columns = [(wide(spread(proj, w, width)), wide(spread(sense, w, width))) for w in range(walkers)]
    groups, parts, spins = [], [], []
    for h in range(rows // PACK):
        group = flag(iota((rows, lanes), 1) // width + PACK * h == iota((rows, lanes), 0))
        cols = dot_exact(feat, group, ((0,), (0,)))
        spins.append(cols[spin_at : spin_at + 1])
        groups.append(group)
        parts.append(thirds(jnp.where(feat_row == spin_at + 1, -3.0, cols) * rate_row))
    for w in range(walkers):
        keep = ((feat_row < spin_at) & (feat_row % walkers == w)) | (feat_row == spin_at + 1)
        for h in range(rows // PACK):
            high, middle, low = [jnp.where(keep, p.astype(F32), 0.0).astype(BF16) for p in parts[h]]
            basis_out[:, tile * lanes : (tile + 1) * lanes] = jnp.concatenate(
                [high, middle, low, high, middle, high], axis=0
            )
            row_proj = jnp.sum(columns[w][0] * groups[h], axis=0, keepdims=True)
            row_sense = jnp.sum(columns[w][1] * groups[h], axis=0, keepdims=True)
            rows_out[8 * tile : 8 * tile + 8] = jnp.concatenate(
                [
                    row_sense,
                    row_proj + bias_low + (1.0 - spins[h]) * bias_step,
                    row_proj + bias_low + spins[h] * bias_step,
                    spins[h],
                    jnp.zeros((4, lanes), F32),
                ],
                axis=0,
            )
            tile += 1


def prepare_row_kernel(walkers, rows, own, w_pair, terms, basis_out, rows_out):
    prepare_kernel(walkers, rows, own, w_pair, terms.at[1:3], terms.at[0:1], basis_out, rows_out)


def fold(x):
    return jnp.sum(x.reshape(x.shape[0] // 8, 8, x.shape[1]), axis=0)


def pair_kernel(walkers, width, rows, total, sets, *refs):
    side, gathered = refs[0], refs[1]
    bigs = refs[2 : 2 + sets]
    bases = refs[2 + sets : 2 + 2 * sets]
    row_sets = refs[2 + 2 * sets : 2 + 3 * sets]
    mix = refs[2 + 3 * sets]
    sens_out, keep_out, send_out, lhs, rhs = refs[3 + 3 * sets :]
    spin_at = 6 * walkers
    feats = spin_at + 8
    lanes = PACK * width
    per_walker = rows // PACK
    tiles = walkers * per_walker
    block = 2 * rows + 8
    starts = [block * s for s in range(gathered.shape[0] // block)]
    proj = jnp.concatenate([gathered[s : s + rows] for s in starts], axis=0)
    sense = jnp.concatenate([gathered[s + rows : s + 2 * rows] for s in starts], axis=0)
    feat = jnp.concatenate(
        [features(gathered[s + 2 * rows : s + block], rows, feats) for s in starts], axis=0
    )
    count = feat.shape[0]
    is_up = jnp.broadcast_to(feat[:, spin_at : spin_at + 1], (count, LANES)) > 0.5
    feat = jnp.where(iota(feat.shape, 1) < feats, feat, 0.0)
    high, middle, low = [p.astype(F32) for p in thirds(feat)]
    first = high + pltpu.roll(high, feats, 1) + pltpu.roll(high, 2 * feats, 1)
    first = first + pltpu.roll(middle, 3 * feats, 1)
    second = middle + pltpu.roll(low, feats, 1)
    left = jnp.concatenate([first, second[:, : 2 * feats]], axis=1).astype(BF16)
    halves = [slice(0, LANES), slice(LANES, lanes)]
    group = 2 * count * per_walker
    sums = [[None] * tiles for _ in range(sets)]
    for w in range(walkers):
        col_proj, col_sense = spread(proj, w, width), spread(sense, w, width)
        for n in range(sets):
            base = (w * sets + n) * group
            for k in range(per_walker):
                tile = w * per_walker + k
                radial = jnp.exp2(dot(left, bases[n][:, tile * lanes : (tile + 1) * lanes]))
                for i, half in enumerate(halves):
                    at = base + (2 * k + i) * count
                    high, low = split(radial[:, half])
                    lhs[at : at + count] = jnp.concatenate([high, low], axis=1)
            mixed = dot(lhs[base : base + group], mix[...])
            mixed = mixed[:, :LANES] + mixed[:, LANES:]
            for k in range(per_walker):
                tile = w * per_walker + k
                acc = []
                for i, half in enumerate(halves):
                    at = (2 * k + i) * count
                    row_sense = row_sets[n][8 * tile : 8 * tile + 1, half]
                    row_base = row_sets[n][8 * tile + 1 : 8 * tile + 2, half]
                    row_turn = row_sets[n][8 * tile + 2 : 8 * tile + 3, half]
                    z = mixed[at : at + count] + col_proj + jnp.where(is_up, row_turn, row_base)
                    if n == 0:
                        owner = iota((rows, LANES), 1) // width + PACK * k + i * (LANES // width)
                        far = jnp.where(owner == iota((rows, LANES), 0), 16384.0, 0.0)
                        z = jnp.concatenate([z[:rows] + far, z[rows:]], axis=0)
                    m = jnp.tanh(z)
                    slope = 1.0 - m * m
                    high, low = split(slope * row_sense)
                    rhs[base + at : base + at + count] = jnp.concatenate([high, low], axis=1)
                    acc.append((fold(slope), fold(jnp.where(is_up, slope, 0.0)), fold(slope * col_sense), fold(m)))
                sums[n][tile] = [jnp.concatenate([a, b], axis=1) for a, b in zip(*acc)]
    tn = ((0,), (0,))
    grams = dot(lhs[...], rhs[...], tn)
    lane8 = iota((8, lanes), 1) // width == iota((8, lanes), 0)
    lane = iota((8, LANES), 1) // width
    sens, mean = [], []
    same_row = jnp.zeros((1, lanes), F32)
    all_row = jnp.zeros((1, lanes), F32)

    def column(row):
        row = jnp.where(lane8, jnp.broadcast_to(row, (8, lanes)), 0.0)
        return ripple(row[:, :LANES] + row[:, LANES:], width)

    for n in range(sets):
        for t in range(tiles):
            slope, turn, col, act = [jnp.sum(x, axis=0, keepdims=True) for x in sums[n][t]]
            row_sense = row_sets[n][8 * t : 8 * t + 1]
            row_spin = row_sets[n][8 * t + 3 : 8 * t + 4]
            own = row_sense * slope
            sens.append(column(own + col))
            mean.append(column(act - 1.0 if n == 0 else act))
            all_row = all_row + own
            same_row = same_row + (1.0 - row_spin) * own
            same_row = same_row + (2.0 * row_spin - 1.0) * (row_sense * turn)
    sens = jnp.concatenate(sens, axis=0)
    mean = jnp.concatenate(mean, axis=0)
    n_rows = walkers * rows
    sens_out[...] = sens[:n_rows]
    lane_all = iota(sens.shape, 1) // width
    both = jnp.where(lane_all == 0, sens, jnp.where(lane_all == 1, mean, 0.0))
    high, low = split(both)
    chunks = (bigs[0].shape[0] - block) // n_rows
    inputs = [
        jnp.concatenate(
            [b[block + k * n_rows : block + (k + 1) * n_rows] for k in range(chunks)], axis=1
        )
        for b in bigs
    ]
    inputs = jnp.concatenate(inputs, axis=0).astype(BF16)
    weights = dot(high, inputs, tn) + dot(low, inputs, tn)
    hidden_width = inputs.shape[1] // 2
    in_part = weights[:width, :hidden_width]
    out_part = weights[width : 2 * width, hidden_width:] / total
    quad = grams[:LANES, :LANES] + grams[LANES:, :LANES] + (grams[:LANES, LANES:] + grams[LANES:, LANES:])
    pair = quad[0:width]
    for k in range(1, LANES // width):
        pair = pair + pltpu.roll(quad[k * width : (k + 1) * width], LANES - k * width, 1)
    tail = jnp.where(lane == 0, pair[0:8], 0.0)
    for k in range(1, width // 8):
        tail = tail + jnp.where(lane == k, pltpu.roll(pair[8 * k : 8 * k + 8], k * width, 1), 0.0)
    pick = iota((8, lanes), 0)
    bias = jnp.where(
        pick == 0,
        jnp.broadcast_to(all_row - same_row, (8, lanes)),
        jnp.where(pick == 1, jnp.broadcast_to(same_row, (8, lanes)), 0.0),
    )
    bias = ripple(bias[:, :LANES] + bias[:, LANES:], width)
    half = hidden_width // 2
    low_half = jnp.concatenate([in_part[:, :half], out_part[:, :half], tail], axis=0)
    high_half = jnp.concatenate([in_part[:, half:], out_part[:, half:], bias], axis=0)
    first = side[0] == 0
    flat = low_half.shape[0]
    keep_out[0:flat] = jnp.where(first, low_half, high_half)
    send_out[...] = jnp.where(first, high_half, low_half)
    place = iota((rows, LANES), 1) // width
    for n in range(1, sets):
        packed = jnp.zeros((rows, LANES), F32)
        for w in range(walkers):
            part = sens[n * n_rows + w * rows : n * n_rows + (w + 1) * rows]
            packed = packed + jnp.where(place == w, part, 0.0)
        at = flat + (n - 1) * rows
        keep_out[at : at + rows] = packed


def hidden_kernel(offsets, sens, w_in, *refs):
    received, grad_out = refs[:-1], refs[-1]
    walkers, rows, _ = grad_out.shape
    width = w_in.shape[0]
    total = []
    for w in range(walkers):
        part = sens[w * rows : (w + 1) * rows]
        for at, ref in zip(offsets, received):
            part = part + spread(ref[at : at + rows], w, width)
        total.append(part)
    high, low = split(jnp.concatenate(total, axis=0))
    both = jnp.concatenate([high[:, :width], low[:, :width]], axis=1)
    grad = dot(both, jnp.concatenate([w_in[...], w_in[...]], axis=0))
    for w in range(walkers):
        grad_out[w] = grad[w * rows : (w + 1) * rows].astype(BF16)


def finish_kernel(side, mine, other, w_in_grad, w_pair_grad, bias_grad, w_out_grad):
    width = w_pair_grad.shape[0]
    first = side[0] == 0
    low = jnp.where(first, mine[...], other[...])
    high = jnp.where(first, other[...], mine[...])
    full = jnp.concatenate([low, high], axis=1)
    w_in_grad[...] = full[:width]
    w_out_grad[...] = full[width : 2 * width]
    tail = full[2 * width :]
    for k in range(width // 8):
        w_pair_grad[8 * k : 8 * k + 8] = tail[:, k * width : (k + 1) * width]
    at = (width // 8) * width
    bias_grad[...] = tail[0:2, at : at + width]


VMEM = pl.BlockSpec(memory_space=pltpu.VMEM)
SMEM = pl.BlockSpec(memory_space=pltpu.SMEM)


def near(x):
    return pltpu.with_memory_space_constraint(x, pltpu.VMEM)


def swap(x, axis, size, mask):
    return lax.ppermute(x, axis, [(i, i ^ mask) for i in range(size)])


def stages(blocks):
    row = min(2, blocks // 2)
    bits = [1 << k for k in range(blocks.bit_length() - 1) if 1 << k != row]
    groups = []
    while len(bits) > 1:
        high, low = bits.pop(), bits.pop()
        groups.append((low, high, low ^ high))
    if bits:
        groups.append((bits.pop(),))
    return groups + [(row,)]


def join(mine, got):
    mine = mine + got[0]
    return mine + (got[1] + got[2]) if len(got) == 3 else mine


def on_device(hidden, cotangent, positions, spins, w_in, w_pair, spin_bias, rates, w_out):
    blocks = lax.axis_size("elec")
    walkers, rows, hidden_width = hidden.shape
    width = w_in.shape[1]
    total = rows * blocks
    block = 2 * rows + 8
    n_rows = walkers * rows
    lanes = PACK * width
    tiles = n_rows // PACK
    groups = stages(blocks)
    col_groups, row_masks = groups[:-1], groups[-1]
    turns = sum(masks[1] for masks in col_groups if len(masks) == 3)
    side = lax.axis_index("walk").astype(jnp.int32)
    for bit in range(blocks.bit_length()):
        if turns >> bit & 1:
            side = side ^ (lax.axis_index("elec").astype(jnp.int32) >> bit & 1)
    side = side.reshape(1)
    sets = 1 + len(row_masks)
    payload, big, *params = pl.pallas_call(
        functools.partial(embed_kernel, total),
        out_shape=(
            pltpu.VMEM((block, LANES), F32),
            pltpu.VMEM((block + n_rows * 2 * hidden_width // LANES, LANES), F32),
            pltpu.VMEM((width, hidden_width), BF16),
            pltpu.VMEM((width, width), F32),
            pltpu.VMEM((2, width), F32),
            pltpu.VMEM((1, width), F32),
        ),
        in_specs=[VMEM] * 9,
        out_specs=(VMEM,) * 6,
        name="embed",
    )(
        hidden,
        cotangent,
        positions.transpose(1, 0, 2),
        spins.reshape(1, rows),
        w_in.T,
        w_out,
        w_pair,
        spin_bias,
        rates.reshape(1, width),
    )
    w_in_near, *params = [near(p) for p in params]
    bigs = [big] + [swap(big, "elec", blocks, m) for m in row_masks]
    gathered = [payload]
    for masks in col_groups:
        whole = gathered[0] if len(gathered) == 1 else jnp.concatenate(gathered, axis=0)
        gathered = [whole] + [swap(whole, "elec", blocks, m) for m in masks]
    columns = gathered[0] if len(gathered) == 1 else jnp.concatenate(gathered, axis=0)
    depth = 6 * (6 * walkers + 8)

    shapes = (pltpu.VMEM((depth, tiles * lanes), BF16), pltpu.VMEM((8 * tiles, lanes), F32))
    basis, row_terms, mix, terms = pl.pallas_call(
        functools.partial(prepare_kernel, walkers, rows),
        out_shape=shapes + (pltpu.VMEM((lanes, lanes), BF16), pltpu.VMEM((3, lanes), F32)),
        in_specs=[VMEM] * 4,
        out_specs=(VMEM,) * 4,
        name="prepare_own",
    )(near(payload), *params)
    bases, row_sets = [basis], [row_terms]
    for source in bigs[1:]:
        basis, row_terms = pl.pallas_call(
            functools.partial(prepare_row_kernel, walkers, rows),
            out_shape=shapes,
            in_specs=[VMEM] * 3,
            out_specs=(VMEM,) * 2,
            name="prepare_row",
        )(near(source), params[0], near(terms))
        bases.append(basis)
        row_sets.append(row_terms)
    flat = 2 * width + 8
    tall = flat + (sets - 1) * rows
    depth = columns.shape[0] // block * rows * 2 * tiles * sets
    operands = [columns, *bigs, *bases, *row_sets, mix]
    sens, keep, send = pl.pallas_call(
        functools.partial(pair_kernel, walkers, width, rows, total, sets),
        out_shape=(
            pltpu.VMEM((n_rows, LANES), F32),
            pltpu.VMEM((tall, LANES), F32),
            pltpu.VMEM((flat, LANES), F32),
        ),
        in_specs=[SMEM] + [VMEM] * len(operands),
        out_specs=(VMEM,) * 3,
        scratch_shapes=[pltpu.VMEM((depth, 2 * LANES), BF16)] * 2,
        name="pairs",
    )(side, *[near(x) for x in operands])
    near_part = swap(send, "walk", 2, 1)
    got = [swap(keep, "elec", blocks, m) for m in row_masks]
    cross = [swap(send, ("elec", "walk"), 2 * blocks, 2 * m + 1) for m in row_masks]
    offsets = tuple(flat + n * rows for n in range(len(got)))
    grad = pl.pallas_call(
        functools.partial(hidden_kernel, offsets),
        out_shape=jax.ShapeDtypeStruct(hidden.shape, BF16),
        in_specs=[VMEM] * (2 + len(got)),
        out_specs=VMEM,
        name="hidden_grad",
    )(near(sens), w_in_near, *[near(g) for g in got])
    mine = join(keep[:flat] + near_part, [g[:flat] + c for g, c in zip(got, cross)])
    for masks in reversed(col_groups):
        got = [
            swap(mine, ("elec", "walk"), 2 * blocks, 2 * m + (m & turns).bit_count() % 2)
            for m in masks
        ]
        mine = join(mine, got)
    other = swap(mine, "walk", 2, 1)
    w_in_grad, w_pair_grad, spin_bias_grad, w_out_grad = pl.pallas_call(
        finish_kernel,
        out_shape=(
            jax.ShapeDtypeStruct((width, hidden_width), F32),
            jax.ShapeDtypeStruct((width, width), F32),
            jax.ShapeDtypeStruct((2, width), F32),
            jax.ShapeDtypeStruct((width, hidden_width), F32),
        ),
        in_specs=[SMEM, VMEM, VMEM],
        out_specs=(VMEM,) * 4,
        name="finish",
    )(side, near(mine), near(other))
    return (grad, w_in_grad.T, w_pair_grad, spin_bias_grad, w_out_grad)


def solution(mesh):
    return jax.shard_map(
        on_device,
        mesh=mesh,
        in_specs=(
            P(("groups", "walk"), "elec", None),
            P(("groups", "walk"), "elec", None),
            P(("groups", "walk"), None, "elec"),
            P(("groups", "elec")),
            P(),
            P(),
            P(),
            P(),
            P(),
        ),
        out_specs=(
            P(("groups", "walk"), "elec", None),
            P("groups", None),
            P("groups", None),
            P("groups", None),
            P("groups", None),
        ),
        check_vma=False,
    )
```

```python
import functools
import math

import jax
import jax.numpy as jnp
from jax import lax
from jax.experimental import pallas as pl
from jax.experimental.pallas import tpu as pltpu
from jax.sharding import PartitionSpec as P


F32, BF16 = jnp.float32, jnp.bfloat16
LANES = 128
PACK = 8


def dot(a, b, dims=((1,), (0,))):
    return lax.dot_general(a, b, (dims, ((), ())), preferred_element_type=F32)


def dot_exact(a, b, dims=((1,), (0,))):
    return lax.dot_general(
        a, b, (dims, ((), ())), precision=lax.Precision.HIGHEST, preferred_element_type=F32
    )


def split(x):
    high = x.astype(BF16)
    return high, (x - high.astype(F32)).astype(BF16)


def iota(shape, axis):
    return lax.broadcasted_iota(jnp.int32, shape, axis)


def flag(condition):
    return jnp.where(condition, 1.0, 0.0).astype(F32)


def embed_kernel(total, hid, cot, pos, spin, w_in, w_out, w_pair, spin_bias, rates, out, big_out, *copies):
    walkers, rows, hidden_width = hid.shape
    proj, sense = [], []
    block = 2 * rows + 8
    n_rows = walkers * rows
    for w in range(walkers):
        proj.append(dot(hid[w], w_in[...], ((1,), (1,))))
        sense.append(dot(cot[w], w_out[...], ((1,), (1,))) / total)
        for k in range(hidden_width // LANES):
            at = block + k * n_rows + w * rows
            big_out[at : at + rows] = hid[w][:, k * LANES : (k + 1) * LANES].astype(F32)
            at = at + hidden_width // LANES * n_rows
            big_out[at : at + rows] = cot[w][:, k * LANES : (k + 1) * LANES].astype(F32)
    feats = []
    for c in range(3):
        x = pos[c]
        feats.append(jnp.cos(jnp.concatenate([x, x - 0.25], axis=0) * (2.0 * jnp.pi)))
    labels = jnp.broadcast_to(spin[...].astype(F32), (8, rows))
    feats.append(jnp.where(iota((8, rows), 0) == 0, labels, 1.0))
    feat = jnp.concatenate(feats, axis=0).T
    parts = [feat[8 * k : 8 * k + 8] for k in range(rows // 8)]
    parts.append(jnp.zeros((8, LANES - feat.shape[1] * (rows // 8)), F32))
    mine = jnp.concatenate(
        [
            jnp.concatenate(proj, axis=1),
            jnp.concatenate(sense, axis=1),
            jnp.concatenate(parts, axis=1),
        ],
        axis=0,
    )
    out[...] = mine
    big_out[0:block] = mine
    for ref, copy in zip((w_in, w_pair, spin_bias, rates), copies):
        copy[...] = ref[...]


def ripple(x, width):
    step = width
    while step < LANES:
        x = x + pltpu.roll(x, step, 1)
        step *= 2
    return x


def spread(x, w, width):
    return ripple(jnp.where(iota(x.shape, 1) // width == w, x, 0.0), width)


def wide(x):
    return jnp.concatenate([x, x], axis=1)


def thirds(x):
    high = x.astype(BF16)
    rest = x - high.astype(F32)
    middle = rest.astype(BF16)
    return high, middle, (rest - middle.astype(F32)).astype(BF16)


def features(packed, rows, feats):
    parts = [packed] + [pltpu.roll(packed, LANES - feats * k, 1) for k in range(1, rows // 8)]
    return jnp.concatenate(parts, axis=0)


def prepare_kernel(walkers, rows, own, w_pair, spin_bias, rates, basis_out, rows_out, *mix_out):
    width = w_pair.shape[0]
    lanes = PACK * width
    spin_at = 6 * walkers
    feats = spin_at + 8
    if mix_out:
        sel = flag(iota((LANES, width), 0) % width == iota((LANES, width), 1)).astype(BF16)
        sel_t = flag(iota((width, LANES), 1) % width == iota((width, LANES), 0)).astype(BF16)
        same = iota((LANES, LANES), 0) // width == iota((LANES, LANES), 1) // width
        high, low = [
            jnp.where(same, dot(dot(sel, part).astype(BF16), sel_t), 0.0) for part in split(w_pair[...])
        ]
        top = jnp.concatenate([high, low], axis=1)
        bottom = jnp.concatenate([high, jnp.zeros_like(high)], axis=1)
        mix_out[0][...] = jnp.concatenate([top, bottom], axis=0).astype(BF16)
    if mix_out:
        sel_wide = flag(iota((width, lanes), 1) % width == iota((width, lanes), 0))
        rate_row = dot_exact(rates[...], sel_wide) * (0.5 / (math.pi**2 * math.log(2.0)))
        bias_rows = dot_exact(spin_bias[...], sel_wide)
        mix_out[1][...] = jnp.concatenate([rate_row, bias_rows], axis=0)
    else:
        rate_row, bias_rows = rates[...], spin_bias[...]
    bias_low, bias_step = bias_rows[0:1], bias_rows[1:2] - bias_rows[0:1]
    proj, sense = own[0:rows], own[rows : 2 * rows]
    feat = features(own[2 * rows : 2 * rows + 8], rows, feats)[:, :feats]
    feat_row = iota((feats, lanes), 0)
    tile = 0
    columns = [(wide(spread(proj, w, width)), wide(spread(sense, w, width))) for w in range(walkers)]
    groups, parts, spins = [], [], []
    for h in range(rows // PACK):
        group = flag(iota((rows, lanes), 1) // width + PACK * h == iota((rows, lanes), 0))
        cols = dot(
            jnp.concatenate(thirds(feat), axis=0),
            jnp.concatenate([group] * 3, axis=0).astype(BF16),
            ((0,), (0,)),
        )
        spins.append(cols[spin_at : spin_at + 1])
        groups.append(group)
        parts.append(thirds(jnp.where(feat_row == spin_at + 1, -3.0, cols) * rate_row))
    for w in range(walkers):
        keep = ((feat_row < spin_at) & (feat_row % walkers == w)) | (feat_row == spin_at + 1)
        for h in range(rows // PACK):
            high, middle, low = [jnp.where(keep, p.astype(F32), 0.0).astype(BF16) for p in parts[h]]
            basis_out[:, tile * lanes : (tile + 1) * lanes] = jnp.concatenate(
                [high, middle, low, high, middle, high], axis=0
            )
            row_proj = jnp.sum(columns[w][0] * groups[h], axis=0, keepdims=True)
            row_sense = jnp.sum(columns[w][1] * groups[h], axis=0, keepdims=True)
            rows_out[8 * tile : 8 * tile + 8] = jnp.concatenate(
                [
                    row_sense,
                    row_proj + bias_low + (1.0 - spins[h]) * bias_step,
                    row_proj + bias_low + spins[h] * bias_step,
                    spins[h],
                    jnp.zeros((4, lanes), F32),
                ],
                axis=0,
            )
            tile += 1


def prepare_row_kernel(walkers, rows, own, w_pair, terms, basis_out, rows_out):
    prepare_kernel(walkers, rows, own, w_pair, terms.at[1:3], terms.at[0:1], basis_out, rows_out)


def fold(x):
    return jnp.sum(x.reshape(x.shape[0] // 8, 8, x.shape[1]), axis=0)


def pair_kernel(walkers, width, rows, total, sets, *refs):
    side, gathered = refs[0], refs[1]
    bigs = refs[2 : 2 + sets]
    bases = refs[2 + sets : 2 + 2 * sets]
    row_sets = refs[2 + 2 * sets : 2 + 3 * sets]
    mix = refs[2 + 3 * sets]
    sens_out, keep_out, send_out, lhs, rhs = refs[3 + 3 * sets :]
    spin_at = 6 * walkers
    feats = spin_at + 8
    lanes = PACK * width
    per_walker = rows // PACK
    tiles = walkers * per_walker
    block = 2 * rows + 8
    starts = [block * s for s in range(gathered.shape[0] // block)]
    proj = jnp.concatenate([gathered[s : s + rows] for s in starts], axis=0)
    sense = jnp.concatenate([gathered[s + rows : s + 2 * rows] for s in starts], axis=0)
    feat = jnp.concatenate(
        [features(gathered[s + 2 * rows : s + block], rows, feats) for s in starts], axis=0
    )
    count = feat.shape[0]
    is_up = jnp.broadcast_to(feat[:, spin_at : spin_at + 1], (count, LANES)) > 0.5
    feat = jnp.where(iota(feat.shape, 1) < feats, feat, 0.0)
    high, middle, low = [p.astype(F32) for p in thirds(feat)]
    first = high + pltpu.roll(high, feats, 1) + pltpu.roll(high, 2 * feats, 1)
    first = first + pltpu.roll(middle, 3 * feats, 1)
    second = middle + pltpu.roll(low, feats, 1)
    left = jnp.concatenate([first, second[:, : 2 * feats]], axis=1).astype(BF16)
    halves = [slice(0, LANES), slice(LANES, lanes)]
    group = 2 * count * per_walker
    sums = [[None] * tiles for _ in range(sets)]
    for w in range(walkers):
        col_proj, col_sense = spread(proj, w, width), spread(sense, w, width)
        for n in range(sets):
            base = (w * sets + n) * group
            for k in range(per_walker):
                tile = w * per_walker + k
                radial = jnp.exp2(dot(left, bases[n][:, tile * lanes : (tile + 1) * lanes]))
                for i, half in enumerate(halves):
                    at = base + (2 * k + i) * count
                    high, low = split(radial[:, half])
                    lhs[at : at + count] = jnp.concatenate([high, low], axis=1)
            mixed = dot(lhs[base : base + group], mix[...])
            mixed = mixed[:, :LANES] + mixed[:, LANES:]
            for k in range(per_walker):
                tile = w * per_walker + k
                acc = []
                for i, half in enumerate(halves):
                    at = (2 * k + i) * count
                    row_sense = row_sets[n][8 * tile : 8 * tile + 1, half]
                    row_base = row_sets[n][8 * tile + 1 : 8 * tile + 2, half]
                    row_turn = row_sets[n][8 * tile + 2 : 8 * tile + 3, half]
                    z = mixed[at : at + count] + col_proj + jnp.where(is_up, row_turn, row_base)
                    if n == 0:
                        owner = iota((rows, LANES), 1) // width + PACK * k + i * (LANES // width)
                        far = jnp.where(owner == iota((rows, LANES), 0), 16384.0, 0.0)
                        z = jnp.concatenate([z[:rows] + far, z[rows:]], axis=0)
                    m = jnp.tanh(z)
                    slope = 1.0 - m * m
                    high, low = split(slope * row_sense)
                    rhs[base + at : base + at + count] = jnp.concatenate([high, low], axis=1)
                    acc.append((fold(slope), fold(jnp.where(is_up, slope, 0.0)), fold(slope * col_sense), fold(m)))
                sums[n][tile] = [jnp.concatenate([a, b], axis=1) for a, b in zip(*acc)]
    tn = ((0,), (0,))
    grams = dot(lhs[...], rhs[...], tn)
    lane8 = iota((8, lanes), 1) // width == iota((8, lanes), 0)
    lane = iota((8, LANES), 1) // width
    sens, mean = [], []
    same_row = jnp.zeros((1, lanes), F32)
    all_row = jnp.zeros((1, lanes), F32)

    def column(row):
        row = jnp.where(lane8, jnp.broadcast_to(row, (8, lanes)), 0.0)
        return ripple(row[:, :LANES] + row[:, LANES:], width)

    for n in range(sets):
        for t in range(tiles):
            slope, turn, col, act = [jnp.sum(x, axis=0, keepdims=True) for x in sums[n][t]]
            row_sense = row_sets[n][8 * t : 8 * t + 1]
            row_spin = row_sets[n][8 * t + 3 : 8 * t + 4]
            own = row_sense * slope
            sens.append(column(own + col))
            mean.append(column(act - 1.0 if n == 0 else act))
            all_row = all_row + own
            same_row = same_row + (1.0 - row_spin) * own
            same_row = same_row + (2.0 * row_spin - 1.0) * (row_sense * turn)
    sens = jnp.concatenate(sens, axis=0)
    mean = jnp.concatenate(mean, axis=0)
    n_rows = walkers * rows
    sens_out[...] = sens[:n_rows]
    lane_all = iota(sens.shape, 1) // width
    both = jnp.where(lane_all == 0, sens, jnp.where(lane_all == 1, mean, 0.0))
    high, low = split(both)
    chunks = (bigs[0].shape[0] - block) // n_rows
    inputs = [
        jnp.concatenate(
            [b[block + k * n_rows : block + (k + 1) * n_rows] for k in range(chunks)], axis=1
        )
        for b in bigs
    ]
    inputs = jnp.concatenate(inputs, axis=0).astype(BF16)
    weights = dot(high, inputs, tn) + dot(low, inputs, tn)
    hidden_width = inputs.shape[1] // 2
    in_part = weights[:width, :hidden_width]
    out_part = weights[width : 2 * width, hidden_width:] / total
    quad = grams[:LANES, :LANES] + grams[LANES:, :LANES] + (grams[:LANES, LANES:] + grams[LANES:, LANES:])
    pair = quad[0:width]
    for k in range(1, LANES // width):
        pair = pair + pltpu.roll(quad[k * width : (k + 1) * width], LANES - k * width, 1)
    tail = jnp.where(lane == 0, pair[0:8], 0.0)
    for k in range(1, width // 8):
        tail = tail + jnp.where(lane == k, pltpu.roll(pair[8 * k : 8 * k + 8], k * width, 1), 0.0)
    pick = iota((8, lanes), 0)
    bias = jnp.where(
        pick == 0,
        jnp.broadcast_to(all_row - same_row, (8, lanes)),
        jnp.where(pick == 1, jnp.broadcast_to(same_row, (8, lanes)), 0.0),
    )
    bias = ripple(bias[:, :LANES] + bias[:, LANES:], width)
    half = hidden_width // 2
    low_half = jnp.concatenate([in_part[:, :half], out_part[:, :half], tail], axis=0)
    high_half = jnp.concatenate([in_part[:, half:], out_part[:, half:], bias], axis=0)
    first = side[0] == 0
    flat = low_half.shape[0]
    keep_out[0:flat] = jnp.where(first, low_half, high_half)
    send_out[...] = jnp.where(first, high_half, low_half)
    place = iota((rows, LANES), 1) // width
    for n in range(1, sets):
        packed = jnp.zeros((rows, LANES), F32)
        for w in range(walkers):
            part = sens[n * n_rows + w * rows : n * n_rows + (w + 1) * rows]
            packed = packed + jnp.where(place == w, part, 0.0)
        at = flat + (n - 1) * rows
        keep_out[at : at + rows] = packed


def hidden_kernel(offsets, sens, w_in, *refs):
    received, grad_out = refs[:-1], refs[-1]
    walkers, rows, _ = grad_out.shape
    width = w_in.shape[0]
    total = []
    for w in range(walkers):
        part = sens[w * rows : (w + 1) * rows]
        for at, ref in zip(offsets, received):
            part = part + spread(ref[at : at + rows], w, width)
        total.append(part)
    high, low = split(jnp.concatenate(total, axis=0))
    both = jnp.concatenate([high[:, :width], low[:, :width]], axis=1)
    grad = dot(both, jnp.concatenate([w_in[...], w_in[...]], axis=0))
    for w in range(walkers):
        grad_out[w] = grad[w * rows : (w + 1) * rows].astype(BF16)


def finish_kernel(side, mine, other, w_in_grad, w_pair_grad, bias_grad, w_out_grad):
    width = w_pair_grad.shape[0]
    first = side[0] == 0
    low = jnp.where(first, mine[...], other[...])
    high = jnp.where(first, other[...], mine[...])
    full = jnp.concatenate([low, high], axis=1)
    w_in_grad[...] = full[:width]
    w_out_grad[...] = full[width : 2 * width]
    tail = full[2 * width :]
    for k in range(width // 8):
        w_pair_grad[8 * k : 8 * k + 8] = tail[:, k * width : (k + 1) * width]
    at = (width // 8) * width
    bias_grad[...] = tail[0:2, at : at + width]


VMEM = pl.BlockSpec(memory_space=pltpu.VMEM)
SMEM = pl.BlockSpec(memory_space=pltpu.SMEM)


def near(x):
    return pltpu.with_memory_space_constraint(x, pltpu.VMEM)


def swap(x, axis, size, mask):
    return lax.ppermute(x, axis, [(i, i ^ mask) for i in range(size)])


def stages(blocks):
    row = min(2, blocks // 2)
    bits = [1 << k for k in range(blocks.bit_length() - 1) if 1 << k != row]
    groups = []
    while len(bits) > 1:
        high, low = bits.pop(), bits.pop()
        groups.append((low, high, low ^ high))
    if bits:
        groups.append((bits.pop(),))
    return groups + [(row,)]


def join(mine, got):
    mine = mine + got[0]
    return mine + (got[1] + got[2]) if len(got) == 3 else mine


def on_device(hidden, cotangent, positions, spins, w_in, w_pair, spin_bias, rates, w_out):
    blocks = lax.axis_size("elec")
    walkers, rows, hidden_width = hidden.shape
    width = w_in.shape[1]
    total = rows * blocks
    block = 2 * rows + 8
    n_rows = walkers * rows
    lanes = PACK * width
    tiles = n_rows // PACK
    groups = stages(blocks)
    col_groups, row_masks = groups[:-1], groups[-1]
    turns = sum(masks[1] for masks in col_groups if len(masks) == 3)
    side = lax.axis_index("walk").astype(jnp.int32)
    for bit in range(blocks.bit_length()):
        if turns >> bit & 1:
            side = side ^ (lax.axis_index("elec").astype(jnp.int32) >> bit & 1)
    side = side.reshape(1)
    sets = 1 + len(row_masks)
    payload, big, *params = pl.pallas_call(
        functools.partial(embed_kernel, total),
        out_shape=(
            pltpu.VMEM((block, LANES), F32),
            pltpu.VMEM((block + n_rows * 2 * hidden_width // LANES, LANES), F32),
            pltpu.VMEM((width, hidden_width), BF16),
            pltpu.VMEM((width, width), F32),
            pltpu.VMEM((2, width), F32),
            pltpu.VMEM((1, width), F32),
        ),
        in_specs=[VMEM] * 9,
        out_specs=(VMEM,) * 6,
        name="embed",
    )(
        hidden,
        cotangent,
        positions.transpose(1, 0, 2),
        spins.reshape(1, rows),
        w_in.T,
        w_out,
        w_pair,
        spin_bias,
        rates.reshape(1, width),
    )
    w_in_near, *params = [near(p) for p in params]
    bigs = [big] + [swap(big, "elec", blocks, m) for m in row_masks]
    gathered = [payload]
    for masks in col_groups:
        whole = gathered[0] if len(gathered) == 1 else jnp.concatenate(gathered, axis=0)
        gathered = [whole] + [swap(whole, "elec", blocks, m) for m in masks]
    columns = gathered[0] if len(gathered) == 1 else jnp.concatenate(gathered, axis=0)
    depth = 6 * (6 * walkers + 8)

    shapes = (pltpu.VMEM((depth, tiles * lanes), BF16), pltpu.VMEM((8 * tiles, lanes), F32))
    basis, row_terms, mix, terms = pl.pallas_call(
        functools.partial(prepare_kernel, walkers, rows),
        out_shape=shapes + (pltpu.VMEM((lanes, lanes), BF16), pltpu.VMEM((3, lanes), F32)),
        in_specs=[VMEM] * 4,
        out_specs=(VMEM,) * 4,
        name="prepare_own",
    )(near(payload), *params)
    bases, row_sets = [basis], [row_terms]
    for source in bigs[1:]:
        basis, row_terms = pl.pallas_call(
            functools.partial(prepare_row_kernel, walkers, rows),
            out_shape=shapes,
            in_specs=[VMEM] * 3,
            out_specs=(VMEM,) * 2,
            name="prepare_row",
        )(near(source), params[0], near(terms))
        bases.append(basis)
        row_sets.append(row_terms)
    flat = 2 * width + 8
    tall = flat + (sets - 1) * rows
    depth = columns.shape[0] // block * rows * 2 * tiles * sets
    operands = [columns, *bigs, *bases, *row_sets, mix]
    sens, keep, send = pl.pallas_call(
        functools.partial(pair_kernel, walkers, width, rows, total, sets),
        out_shape=(
            pltpu.VMEM((n_rows, LANES), F32),
            pltpu.VMEM((tall, LANES), F32),
            pltpu.VMEM((flat, LANES), F32),
        ),
        in_specs=[SMEM] + [VMEM] * len(operands),
        out_specs=(VMEM,) * 3,
        scratch_shapes=[pltpu.VMEM((depth, 2 * LANES), BF16)] * 2,
        name="pairs",
    )(side, *[near(x) for x in operands])
    near_part = swap(send, "walk", 2, 1)
    got = [swap(keep, "elec", blocks, m) for m in row_masks]
    cross = [swap(send, ("elec", "walk"), 2 * blocks, 2 * m + 1) for m in row_masks]
    offsets = tuple(flat + n * rows for n in range(len(got)))
    grad = pl.pallas_call(
        functools.partial(hidden_kernel, offsets),
        out_shape=jax.ShapeDtypeStruct(hidden.shape, BF16),
        in_specs=[VMEM] * (2 + len(got)),
        out_specs=VMEM,
        name="hidden_grad",
    )(near(sens), w_in_near, *[near(g) for g in got])
    mine = join(keep[:flat] + near_part, [g[:flat] + c for g, c in zip(got, cross)])
    for masks in reversed(col_groups):
        got = [
            swap(mine, ("elec", "walk"), 2 * blocks, 2 * m + (m & turns).bit_count() % 2)
            for m in masks
        ]
        mine = join(mine, got)
    other = swap(mine, "walk", 2, 1)
    w_in_grad, w_pair_grad, spin_bias_grad, w_out_grad = pl.pallas_call(
        finish_kernel,
        out_shape=(
            jax.ShapeDtypeStruct((width, hidden_width), F32),
            jax.ShapeDtypeStruct((width, width), F32),
            jax.ShapeDtypeStruct((2, width), F32),
            jax.ShapeDtypeStruct((width, hidden_width), F32),
        ),
        in_specs=[SMEM, VMEM, VMEM],
        out_specs=(VMEM,) * 4,
        name="finish",
    )(side, near(mine), near(other))
    return (grad, w_in_grad.T, w_pair_grad, spin_bias_grad, w_out_grad)


def solution(mesh):
    return jax.shard_map(
        on_device,
        mesh=mesh,
        in_specs=(
            P(("groups", "walk"), "elec", None),
            P(("groups", "walk"), "elec", None),
            P(("groups", "walk"), None, "elec"),
            P(("groups", "elec")),
            P(),
            P(),
            P(),
            P(),
            P(),
        ),
        out_specs=(
            P(("groups", "walk"), "elec", None),
            P("groups", None),
            P("groups", None),
            P("groups", None),
            P("groups", None),
        ),
        check_vma=False,
    )
```
